32 devices in a mesh: tg: 4 (over y, x), tile: 8 (over z, core).
Axes of the slice: x: 2, y: 2, z: 4, core: 2. Of those that a mesh axis runs over, the one named last changes fastest.
Arguments:
- age_cell: int32 [4, 524288], P('tg', 'tile'), may hold values from 0 to 127
- dur_cell: int32 [4, 524288], P('tg', 'tile'), may hold values from 0 to 3
- trans_code: int32 [4, 524288], P('tg', 'tile'), may hold values from 0 to 15
- age_frac: float32 [4, 524288], P('tg', 'tile'), may hold values from 0 to 1
- dur_frac: float32 [4, 524288], P('tg', 'tile'), may hold values from 0 to 1
- exposure: float32 [4, 524288], P('tg', 'tile'), may hold values from 0.05 to 1
- claims: float32 [4, 524288], P('tg', 'tile'), may hold values from 0.01 to 1
- block_tile: int32 [4, 4096, 1], P('tg', 'tile'), may hold values from 0 to 7; in each aligned block of 512 rows (0 to 511, 512 to 1023, ..., all dimensions but the last counted through in order) at most 128 rows name the same one
- smooth_age: float32 [64], P('tg'), may hold values from 0.5 to 8
- smooth_dur: float32 [64], P('tg'), may hold values from 0.5 to 8
- credibility: float32 [64], P('tg'), may hold values from 0.2 to 2
Outputs:
- smoothed: float32 [64, 32, 128], P('tg', 'tile')
- residual: float32 [64, 32, 128], P('tg', 'tile')
The draws below stay inside these ranges and needn't reach their ends.
Inputs may be any that keep to these rules, and one draw needn't show every extreme that they name: `block_tile`: among the 512 blocks of one device, no tile is named by more than 128 blocks.
All inputs are finite; a program needn't handle non-finite values.
Results may differ from the reference program's by a relative error of at most 0.0074.
Values sent between devices are 32-bit elements; how exact they have to be, the bound alone decides.
No kernel may reach another device: no remote copies, remote signals or barrier semaphores. Data moves between devices by JAX's collectives and lax.ppermute only.
A program may use at most 64 MiB of HBM per device.

```python
import math
import jax
import jax.numpy as jnp
import numpy as np
from jax import lax

TRANS = 64
AGE = 128
DT = 4
ITERS = 4
TR_DEV = 16
DUR = 32
BLOCKS_DEV = 512
RECORDS = 524288
CAP = 128
N_TG = 4
N_TILE = 8


def touch_ends(result, own_key, smallest, high):
    longest = result.shape.index(max(result.shape))
    spots = []
    for shift in (0, 1):
        where = [jax.random.randint(jax.random.fold_in(own_key, axis), (), 0, length) for axis, length in enumerate(result.shape)]
        where[longest] = (where[longest] + shift) % result.shape[longest]
        spots.append(tuple(where))
    return result.at[spots[0]].set(smallest).at[spots[1]].set(high)


def shard_levels(stream_key, dims, pieces, least, largest):
    factor_of = 1.0
    for dim, shards_of in pieces:
        heights = jax.random.uniform(jax.random.fold_in(jax.random.fold_in(stream_key, 6), dim), (shards_of,), jnp.float32, least / len(pieces), largest / len(pieces))
        factor_of = factor_of * jnp.repeat(jnp.exp(heights), dims[dim] // shards_of).reshape((-1,) + (1,) * (len(dims) - 1 - dim))
    return factor_of


def shared_out(key, own, number, rows, amount, top, most, skew):
    sequence = jax.random.permutation(key, amount)
    crowded, usual = portions_of(amount, rows * top, most, skew, True), portions_of(amount, rows * top, most, skew, False)
    places = jnp.arange(amount)

    def named(tallies, offset_by):
        used = int((tallies > 0).sum())
        fixed = max(1, used // 4)
        moved = fixed + (places - fixed + offset_by * (used - fixed)) % max(1, amount - fixed)
        return jnp.zeros((amount,), jnp.int32).at[sequence[jnp.where(places < fixed, places, moved)]].set(jnp.asarray(tallies, jnp.int32))

    tallies = jnp.where(number % 4 == 0, named(crowded, number // 4), named(usual, number - number // 4 - 1))
    mixed = jax.random.permutation(jax.random.fold_in(own, 3), amount)
    donor, taker = mixed[0:amount // 2 * 2:2], mixed[1:amount // 2 * 2:2]
    margin = jnp.minimum(tallies[donor] - 1, most - tallies[taker]) // 2
    margin = jnp.where((donor == sequence[0]) | (taker == sequence[0]) | (tallies[taker] == 0), 0, jnp.maximum(margin, 0))
    moved = jax.random.randint(jax.random.fold_in(own, 4), (amount // 2,), 0, 1 << 20) % (margin + 1)
    tallies = tallies.at[donor].add(-moved).at[taker].add(moved)
    items = jnp.searchsorted(jnp.cumsum(tallies), jnp.arange(rows * top), side="right").astype(jnp.int32)
    table = items.reshape(top, rows).T
    table = table[jax.random.permutation(jax.random.fold_in(own, 1), rows)]
    offset_by = jax.random.randint(jax.random.fold_in(own, 2), (rows, 1), 0, top)
    return jnp.take_along_axis(table, (jnp.arange(top)[None, :] + offset_by) % top, axis=1)


def portions_of(number_of, total, most, lean, full):
    loads = [(1 << 20) // math.isqrt(rank ** lean) + 1 for rank in range(1, number_of + 1)]
    largest = most if full else min(most, max(-(-total // number_of), total * loads[0] // sum(loads)))
    least = 1 if total - largest >= number_of - 1 else 0
    counts, surplus = [largest] + [least] * (number_of - 1), total - largest - least * (number_of - 1)
    while surplus > 0:
        candidates = [i for i in range(1, number_of) if counts[i] < largest] or [i for i in range(1, number_of) if counts[i] < most]
        mass, budget = sum([loads[i] for i in candidates]), surplus
        for i in candidates:
            extra = min(most - counts[i], max(1, budget * loads[i] // mass), surplus)
            counts[i] = counts[i] + extra
            surplus = surplus - extra
    return np.array(counts)


def setup_inputs(seed: int = 0) -> dict:
    streams_of = jax.random.split(jax.random.key(seed), 12)
    age_cell = touch_ends(jax.random.randint(streams_of[0], (N_TG, RECORDS), 0, AGE), jax.random.fold_in(streams_of[0], 1), 0, AGE - 1).astype(jnp.int32)
    dur_cell = touch_ends(jax.random.randint(streams_of[1], (N_TG, RECORDS), 0, DT), jax.random.fold_in(streams_of[1], 1), 0, DT - 1).astype(jnp.int32)
    trans_code = touch_ends(jax.random.randint(streams_of[2], (N_TG, RECORDS), 0, TR_DEV), jax.random.fold_in(streams_of[2], 1), 0, TR_DEV - 1).astype(jnp.int32)
    age_frac = jnp.clip(1.0 * jax.random.uniform(streams_of[3], (N_TG, RECORDS), jnp.float32) ** shard_levels(streams_of[3], (N_TG, RECORDS), ((0, 4), (1, 8)), -0.2, 0.2), 0.0, 1.0)
    dur_frac = jnp.clip(1.0 * jax.random.uniform(streams_of[4], (N_TG, RECORDS), jnp.float32) ** shard_levels(streams_of[4], (N_TG, RECORDS), ((0, 4), (1, 8)), -0.2, 0.2), 0.0, 1.0)
    exposure = jnp.clip(jnp.exp(math.log(1.0) - 2.9957323 * jax.random.uniform(streams_of[5], (N_TG, RECORDS), jnp.float32) ** shard_levels(streams_of[5], (N_TG, RECORDS), ((0, 4), (1, 8)), -0.2, 0.2)), 0.05, 1.0)
    claims = jnp.clip(jnp.exp(math.log(1.0) - 4.6051702 * jax.random.uniform(streams_of[6], (N_TG, RECORDS), jnp.float32) ** shard_levels(streams_of[6], (N_TG, RECORDS), ((0, 4), (1, 8)), -0.2, 0.2)), 0.01, 1.0)
    block_tile_keys = jax.random.split(jax.random.fold_in(streams_of[7], 1), N_TG * (BLOCKS_DEV * N_TILE) // BLOCKS_DEV)
    block_tile_turns = jax.random.permutation(jax.random.fold_in(streams_of[7], 3), N_TG * (BLOCKS_DEV * N_TILE) // BLOCKS_DEV)
    block_tile = jax.vmap(lambda own, number: shared_out(jax.random.fold_in(streams_of[7], 2), own, number, BLOCKS_DEV, N_TILE, 1, CAP, 2))(block_tile_keys, block_tile_turns).reshape((N_TG, BLOCKS_DEV * N_TILE, 1))
    smooth_age = jnp.clip(jnp.exp(math.log(8.0) - 2.7725887 * jax.random.uniform(streams_of[8], (TRANS,), jnp.float32) ** shard_levels(streams_of[8], (TRANS,), ((0, 4),), -0.2, 0.2)), 0.5, 8.0)
    smooth_dur = jnp.clip(jnp.exp(math.log(8.0) - 2.7725887 * jax.random.uniform(streams_of[9], (TRANS,), jnp.float32) ** shard_levels(streams_of[9], (TRANS,), ((0, 4),), -0.2, 0.2)), 0.5, 8.0)
    credibility = jnp.clip(jnp.exp(math.log(2.0) - 2.3025851 * jax.random.uniform(streams_of[10], (TRANS,), jnp.float32) ** shard_levels(streams_of[10], (TRANS,), ((0, 4),), -0.2, 0.2)), 0.2, 2.0)
    return dict(age_cell=age_cell, dur_cell=dur_cell, trans_code=trans_code, age_frac=age_frac, dur_frac=dur_frac, exposure=exposure, claims=claims, block_tile=block_tile, smooth_age=smooth_age, smooth_dur=smooth_dur, credibility=credibility)


def spline(frac):
    rest = 1.0 - frac
    cube = frac * frac * frac
    return (rest * rest * rest / 6.0, (3.0 * cube - 6.0 * frac * frac + 4.0) / 6.0, (-3.0 * cube + 3.0 * frac * frac + 3.0 * frac + 1.0) / 6.0, cube / 6.0)


def penalty_matrix(padded_grid, axis, first, record_count):
    inner_product = padded_grid.shape[axis] - 2
    def part(array, lower, length):
        return lax.slice_in_dim(array, lower, lower + length, axis=axis)
    differenced_values = part(padded_grid, 0, inner_product) - 2.0 * part(padded_grid, 1, inner_product) + part(padded_grid, 2, inner_product)
    layout = [1] * padded_grid.ndim
    layout[axis] = inner_product
    place_indices = first - 2 + lax.iota(jnp.int32, inner_product).reshape(layout)
    differenced_values = jnp.where((place_indices >= 0) & (place_indices <= record_count - 3), differenced_values, 0.0)
    final_result = inner_product - 2
    return part(differenced_values, 2, final_result) - 2.0 * part(differenced_values, 1, final_result) + part(differenced_values, 0, final_result)


def rounded(value):
    return lax.optimization_barrier(value.astype(jnp.bfloat16)).astype(jnp.float32)


def reference(age_cell, dur_cell, trans_code, age_frac, dur_frac, exposure, claims, block_tile, smooth_age, smooth_dur, credibility):
    tiles = jnp.repeat(block_tile[:, :, 0], 128, axis=1)
    duration = (tiles * DT + dur_cell).reshape(-1)
    transition = (lax.iota(jnp.int32, N_TG)[:, None] * TR_DEV + trans_code).reshape(-1)
    ages = age_cell.reshape(-1)
    age_w = spline(age_frac.reshape(-1))
    dur_w = spline(dur_frac.reshape(-1))
    values = (exposure.reshape(-1), claims.reshape(-1))
    rows_pad = DUR + 3
    cols_pad = AGE + 3
    flat = jnp.zeros((2 * TRANS * rows_pad * cols_pad,), jnp.float32)
    base = (transition * rows_pad + duration) * cols_pad + ages
    for channel in range(2):
        for place_d in range(4):
            left = rounded(dur_w[place_d] * values[channel])
            for place_a in range(4):
                index = channel * TRANS * rows_pad * cols_pad + base + place_d * cols_pad + place_a
                flat = flat.at[index].add(left * rounded(age_w[place_a]))
    grid = flat.reshape(2, TRANS, rows_pad, cols_pad)[:, :, 1:DUR + 1, 1:AGE + 1]
    expo_grid = grid[0]
    claim_grid = grid[1]
    prior = jnp.sum(claim_grid, axis=0) / (1.0 + jnp.sum(expo_grid, axis=0))
    weight_a = smooth_age[:, None, None]
    weight_d = smooth_dur[:, None, None]
    cred = credibility[:, None, None]
    diagonal = expo_grid + cred

    def operate(field):
        along_age = penalty_matrix(jnp.pad(field, ((0, 0), (0, 0), (2, 2))), 2, 0, AGE)
        along_dur = penalty_matrix(jnp.pad(field, ((0, 0), (2, 2), (0, 0))), 1, 0, DUR)
        return diagonal * field + weight_a * along_age + weight_d * along_dur

    right_side = claim_grid + cred * prior[None]
    smoothed = jnp.zeros_like(right_side)
    residual = right_side
    direction = right_side
    norm_now = jnp.sum(residual * residual, axis=(1, 2))
    for turn in range(ITERS):
        image = operate(direction)
        alpha = norm_now / jnp.sum(direction * image, axis=(1, 2))
        smoothed = smoothed + alpha[:, None, None] * direction
        residual = residual - alpha[:, None, None] * image
        norm_next = jnp.sum(residual * residual, axis=(1, 2))
        direction = residual + (norm_next / norm_now)[:, None, None] * direction
        norm_now = norm_next
    return smoothed, residual
```

```python
import functools

import jax
import jax.numpy as jnp
from jax import lax
from jax.experimental import pallas as pl
from jax.experimental.pallas import tpu as pltpu
from jax.sharding import PartitionSpec as P

AGE = 128
DT = 4
ITERS = 4
LANES = 128
WIN = DT + 3
MXU = 256
STEP = 8
SHARE = 4
ROWS = 2 * WIN * 16


f32 = jnp.float32
bf16 = jnp.bfloat16


def spline(frac):
    rest = 1.0 - frac
    cube = frac * frac * frac
    return (
        rest * rest * rest / 6.0,
        (3.0 * cube - 6.0 * frac * frac + 4.0) / 6.0,
        (-3.0 * cube + 3.0 * frac * frac + 3.0 * frac + 1.0) / 6.0,
        cube / 6.0,
    )


def spread_body(
    blocks,
    tiles,
    core_ref,
    tile_ref,
    age_ref,
    off_ref,
    code_ref,
    age_frac_ref,
    dur_frac_ref,
    expo_ref,
    claim_ref,
    keep_ref,
    send_ref,
    base_s,
    group_s,
    code_s,
    weight_s,
    term_s,
    acc_s,
    order_s,
    fill_s,
):
    slab = 8
    cap = blocks + STEP
    dur = tiles * DT

    def clear(t, _):
        fill_s[t] = 0
        return 0

    lax.fori_loop(0, tiles, clear, 0)
    acc_s[...] = jnp.zeros_like(acc_s)
    blank = jnp.zeros((slab, LANES), f32)
    pad = pl.ds(blocks, slab)
    base_s[pad] = blank
    group_s[pad] = blank
    code_s[pad] = blank - 1.0
    for place in range(4):
        weight_s[place, pad] = blank
    for row in range(2 * WIN):
        term_s[row, pad] = blank

    def prepare(i, _):
        rows = pl.ds(pl.multiple_of(i * slab, slab), slab)
        first = age_ref[rows] - 1
        base_s[rows] = (first & 15).astype(f32)
        group_s[rows] = (first >> 4).astype(f32)
        code_s[rows] = code_ref[rows].astype(f32)
        for place, weight in enumerate(spline(age_frac_ref[rows])):
            weight_s[place, rows] = weight.astype(bf16).astype(f32)
        dur_w = spline(dur_frac_ref[rows])
        offset = off_ref[rows]
        is_offset = [offset == o for o in range(DT)]
        for channel, value in enumerate((expo_ref[rows], claim_ref[rows])):
            terms = [(w * value).astype(bf16).astype(f32) for w in dur_w]
            for cell in range(WIN):
                term = jnp.zeros((slab, LANES), f32)
                for o in range(DT):
                    if 0 <= cell - o < 4:
                        term = jnp.where(is_offset[o], terms[cell - o], term)
                term_s[channel * WIN + cell, rows] = term
        for j in range(slab):
            block = i * slab + j
            t = tile_ref[block]
            count = fill_s[t]
            order_s[t * cap + count] = block
            fill_s[t] = count + 1
        return 0

    lax.fori_loop(0, blocks // slab, prepare, 0)

    row16 = lax.broadcasted_iota(jnp.int32, (16, LANES), 0)
    row16b = row16.astype(f32).astype(bf16)
    codes = [
        (half * 8 + (row16 >> 3) * 4 + (row16 & 3)).astype(f32).astype(bf16) for half in range(2)
    ]
    is_claim = lax.broadcasted_iota(jnp.int32, (8, LANES), 0) >= 4
    zero = jnp.zeros((16, LANES), bf16)
    fill_rows = jnp.zeros((MXU - ROWS, LANES), bf16)

    def spread_row(ref, r, count=16):
        return jnp.broadcast_to(ref[pl.ds(r, 1), :], (count, LANES))

    def build(r):
        base = spread_row(base_s, r).astype(bf16)
        group = spread_row(group_s, r).astype(bf16)
        weights = [spread_row(weight_s.at[place], r).astype(bf16) for place in range(4)]
        ahead = row16b - base
        wraps = ahead < 0
        place = jnp.where(wraps, ahead + 16, ahead)
        pattern = zero
        for k in range(4):
            pattern = jnp.where(place == k, weights[k], pattern)
        owner = jnp.where(wraps, group + 1, group)
        ages = [jnp.where(owner == a, pattern, zero) for a in range(AGE // 16)]
        code = spread_row(code_s, r).astype(bf16)
        masks = [code == c for c in codes]
        left = [[], []]
        for cell in range(WIN):
            expo = spread_row(term_s.at[cell], r, 8)
            claim = spread_row(term_s.at[WIN + cell], r, 8)
            both = jnp.where(is_claim, claim, expo)
            both = jnp.concatenate([both, both], axis=0).astype(bf16)
            for half in range(2):
                left[half].append(jnp.where(masks[half], both, zero))
        return (
            jnp.concatenate(left[0] + left[1] + [fill_rows], axis=0),
            jnp.concatenate(ages, axis=0),
        )

    def all_tiles(acc0, acc1):
        accs = (acc0, acc1)

        def one_tile(t, _):
            count = fill_s[t]
            for j in range(STEP - 1):
                order_s[t * cap + count + j] = blocks

            def step(s, _):
                for pair in range(STEP // 2):
                    at = t * cap + s * STEP + pair * 2
                    left0, ages0 = build(order_s[at])
                    left1, ages1 = build(order_s[at + 1])
                    unit, stage = pair % 2, (pair // 2) % 2
                    pltpu.matmul_push_rhs(
                        jnp.concatenate([left0, left1], axis=1), stage, unit, transpose=True
                    )
                    pltpu.matmul_acc_lhs(
                        accs[unit], jnp.concatenate([ages0, ages1], axis=1), load_staged_rhs=stage
                    )
                return 0

            @pl.when(count > 0)
            def _():
                lax.fori_loop(0, lax.div(count + (STEP - 1), STEP), step, 0)
                total = (pltpu.matmul_pop(acc0) + pltpu.matmul_pop(acc1)).T
                total = total[:ROWS].reshape(2, WIN, 2, 8, LANES)
                for half in range(2):
                    for cell in range(WIN):
                        for quarter in range(2):
                            acc_s[half * 2 + quarter, t * DT + cell] += total[half, cell, quarter]

            return 0

        lax.fori_loop(0, tiles, one_tile, 0)

    pl.run_scoped(all_tiles, pltpu.ACC(0)((AGE, MXU), f32), pltpu.ACC(1)((AGE, MXU), f32))

    mine = core_ref[0]
    for quarter in range(2):
        keep_ref[quarter] = acc_s[mine * 2 + quarter, 1 : dur + 1]
        send_ref[pl.ds(quarter * dur, dur)] = acc_s[(1 - mine) * 2 + quarter, 1 : dur + 1]
    total = jnp.sum(acc_s[:, 1 : dur + 1], axis=0)
    for channel in range(2):
        pooled = jnp.sum(total[:, channel * 4 : channel * 4 + 4], axis=1)
        base = 2 * dur + channel * (dur // 8)
        send_ref[pl.ds(base, dur // 8)] = pooled.reshape(dur // 8, 8, LANES)


def spread(core, tile_ids, fields, tiles):
    blocks = tile_ids.shape[0]
    dur = tiles * DT
    rows = blocks + 8
    vmem = pl.BlockSpec(memory_space=pltpu.VMEM)
    smem = pl.BlockSpec(memory_space=pltpu.SMEM)
    return pl.pallas_call(
        functools.partial(spread_body, blocks, tiles),
        out_shape=(
            jax.ShapeDtypeStruct((2, dur, 8, LANES), f32),
            jax.ShapeDtypeStruct((2 * dur + 2 * (dur // 8), 8, LANES), f32),
        ),
        in_specs=[smem, smem] + [vmem] * 7,
        out_specs=(vmem, vmem),
        scratch_shapes=[
            pltpu.VMEM((rows, LANES), f32),
            pltpu.VMEM((rows, LANES), f32),
            pltpu.VMEM((rows, LANES), f32),
            pltpu.VMEM((4, rows, LANES), f32),
            pltpu.VMEM((2 * WIN, rows, LANES), f32),
            pltpu.VMEM((4, dur + 3, 8, LANES), f32),
            pltpu.SMEM((tiles * (blocks + STEP),), jnp.int32),
            pltpu.SMEM((tiles,), jnp.int32),
        ],
        compiler_params=pltpu.CompilerParams(vmem_limit_bytes=48 * 1024 * 1024),
        name="spread",
    )(core, tile_ids, *fields)


def smooth_body(
    dur,
    where_ref,
    age_w_ref,
    dur_w_ref,
    cred_ref,
    grid_a_ref,
    grid_b_ref,
    pool_a_ref,
    pool_b_ref,
    out_ref,
    prior_s,
    x_s,
    r_s,
):
    half = dur // 2
    slot, high = where_ref[0], where_ref[1]
    sub = lax.broadcasted_iota(jnp.int32, (8, LANES), 0)
    lane = lax.broadcasted_iota(jnp.int32, (1, 8, LANES), 2)
    low = sub < 4

    def swap(v):
        return pltpu.roll(v, 4, v.ndim - 2)

    def per_transition(ref):
        value = jnp.full((8, LANES), ref[slot], f32)
        for t in range(1, 4):
            value = jnp.where((sub & 3) == t, ref[slot + t], value)
        return value

    weight_a, weight_d, cred = map(per_transition, (age_w_ref, dur_w_ref, cred_ref))
    pool = pool_a_ref[...] + pool_b_ref[...]
    eighth = dur // 8
    prior_s[...] = (pool[eighth:] / (1.0 + pool[:eighth])).reshape(dur, LANES)
    grid = grid_a_ref[...] + grid_b_ref[...]
    top, bottom = grid[:half], grid[half:]
    diagonal = jnp.where(low, top, swap(bottom)) + cred
    claims = jnp.where(low, swap(top), bottom)
    prior = jnp.stack(
        [
            jnp.where(
                low,
                jnp.broadcast_to(prior_s[pl.ds(d, 1), :], (8, LANES)),
                jnp.broadcast_to(prior_s[pl.ds(half + d, 1), :], (8, LANES)),
            )
            for d in range(half)
        ]
    )
    rhs = claims + cred * prior

    def operate(v):
        y = v - 2.0 * pltpu.roll(v, LANES - 1, 2) + pltpu.roll(v, LANES - 2, 2)
        y = jnp.where(lane < AGE - 2, y, 0.0)
        along_age = y - 2.0 * pltpu.roll(y, 1, 2) + pltpu.roll(y, 2, 2)
        longer = jnp.concatenate([v, swap(v[:2])], axis=0)
        y = longer[:half] - 2.0 * longer[1 : half + 1] + longer[2 : half + 2]
        y = jnp.concatenate([y[: half - 2], jnp.where(low, y[half - 2 :], 0.0)], axis=0)
        longer = jnp.concatenate([jnp.where(low, 0.0, swap(y[half - 2 :])), y], axis=0)
        along_dur = longer[2:] - 2.0 * longer[1 : half + 1] + longer[:half]
        return diagonal * v + weight_a * along_age + weight_d * along_dur

    def inner(a, b):
        part = jnp.sum(a * b, axis=0)
        part = part + swap(part)
        return jnp.sum(part, axis=1, keepdims=True)

    x = jnp.zeros_like(rhs)
    r = rhs
    p = rhs
    norm = inner(r, r)
    for turn in range(ITERS):
        image = operate(p)
        alpha = norm / inner(p, image)
        x = x + alpha * p
        r = r - alpha * image
        if turn < ITERS - 1:
            after = inner(r, r)
            p = r + (after / norm) * p
            norm = after
    x_s[...] = x
    r_s[...] = r
    span = SHARE * DT
    in_low = high * span < half
    start = jnp.where(in_low, high * span, high * span - half)
    for dest in range(SHARE):
        for d in range(DT):
            xv = x_s[start + dest * DT + d]
            rv = r_s[start + dest * DT + d]
            row = jnp.where(
                in_low, jnp.where(low, xv, swap(rv)), jnp.where(low, swap(xv), rv)
            )
            out_ref[dest, pl.ds(d, 8, stride=DT), :] = row


def smooth(where, weights, grid_a, grid_b, pool_a, pool_b):
    dur = grid_a.shape[0]
    vmem = pl.BlockSpec(memory_space=pltpu.VMEM)
    smem = pl.BlockSpec(memory_space=pltpu.SMEM)
    return pl.pallas_call(
        functools.partial(smooth_body, dur),
        out_shape=jax.ShapeDtypeStruct((SHARE, 8 * DT, LANES), f32),
        in_specs=[smem] * 4 + [vmem] * 4,
        out_specs=vmem,
        scratch_shapes=[
            pltpu.VMEM((dur, LANES), f32),
            pltpu.VMEM((dur // 2, 8, LANES), f32),
            pltpu.VMEM((dur // 2, 8, LANES), f32),
        ],
        compiler_params=pltpu.CompilerParams(vmem_limit_bytes=32 * 1024 * 1024),
        name="smooth",
    )(where, *weights, grid_a, grid_b, pool_a, pool_b)


def gather_body(me_ref, own_ref, one_ref, two_ref, three_ref, x_ref, r_ref):
    me = me_ref[0]
    for k, ref in enumerate((own_ref, one_ref, two_ref, three_ref)):
        other = me ^ k
        slot = (other & 1) * 2 + (other >> 1)
        got = ref[me] if k == 0 else ref[...]
        x_ref[slot] = got[: 4 * DT]
        r_ref[slot] = got[4 * DT :]


def gather(me, own, others):
    vmem = pl.BlockSpec(memory_space=pltpu.VMEM)
    smem = pl.BlockSpec(memory_space=pltpu.SMEM)
    shape = jax.ShapeDtypeStruct((SHARE, 4 * DT, LANES), f32)
    return pl.pallas_call(
        gather_body,
        out_shape=(shape, shape),
        in_specs=[smem] + [vmem] * 4,
        out_specs=(vmem, vmem),
        name="gather",
    )(me, own, *others)


def swap_with(value, axis, bit):
    size = lax.axis_size(axis)
    return lax.ppermute(value, axis, [(i, i ^ bit) for i in range(size)])


def bits_of(size):
    bits = [1 << k for k in range(size.bit_length() - 1)]
    assert 1 << len(bits) == size, size
    return bits


def per_device(
    age_cell,
    dur_cell,
    trans_code,
    age_frac,
    dur_frac,
    exposure,
    claims,
    block_tile,
    smooth_age,
    smooth_dur,
    credibility,
):
    trans_dev = smooth_age.shape[0]
    tiles = lax.axis_size("tile")
    groups = lax.axis_size("tg")
    dur = tiles * DT
    assert trans_dev == 4 * SHARE and tiles % 8 == 0
    here = lax.axis_index("tile")
    core, near, high = here & 1, (here >> 1) & 1, here >> 2
    tile_ids = block_tile.reshape(-1)
    blocks = tile_ids.shape[0]
    fields = [
        field.reshape(blocks, LANES)
        for field in (age_cell, dur_cell, trans_code, age_frac, dur_frac, exposure, claims)
    ]
    keep, send = spread(core.reshape(1), tile_ids, fields, tiles)
    got = swap_with(send, "tile", 1)
    pool = send[2 * dur :] + got[2 * dur :]
    got = got[: 2 * dur].reshape(keep.shape)

    def quarter(at):
        return lax.dynamic_index_in_dim(keep, at, 0, False) + lax.dynamic_index_in_dim(
            got, at, 0, False
        )

    grid = quarter(near) + swap_with(quarter(1 - near), "tile", 2)
    tile_bits = bits_of(tiles)
    pool_bits = [("tg", bit) for bit in bits_of(groups)] + [("tile", bit) for bit in tile_bits[1:]]
    for axis, bit in pool_bits[:-1]:
        pool = pool + swap_with(pool, axis, bit)
    pool_other = swap_with(pool, *pool_bits[-1])
    for bit in tile_bits[2:-1]:
        grid = grid + swap_with(grid, "tile", bit)
    grid_other = swap_with(grid, "tile", tile_bits[-1])
    slot = core * 8 + near * 4
    own = smooth(
        jnp.stack([slot, high]),
        (smooth_age, smooth_dur, credibility),
        grid,
        grid_other,
        pool,
        pool_other,
    )
    me = here & 3
    others = [
        swap_with(lax.dynamic_index_in_dim(own, me ^ k, 0, False), "tile", k) for k in (1, 2, 3)
    ]
    smoothed, residual = gather(me.reshape(1), own, others)
    shape = (trans_dev, DT, AGE)
    return smoothed.reshape(shape), residual.reshape(shape)


def solution(mesh):
    records = P("tg", "tile")
    in_specs = (records,) * 7 + (P("tg", "tile", None),) + (P("tg"),) * 3
    out_specs = (P("tg", "tile", None), P("tg", "tile", None))
    mapped = jax.shard_map(
        per_device, mesh=mesh, in_specs=in_specs, out_specs=out_specs, check_vma=False
    )

    def run(*args):
        with jax.sharding.use_abstract_mesh(mesh.abstract_mesh):
            return mapped(*args)

    return run
```

```python
import functools

import jax
import jax.numpy as jnp
from jax import lax
from jax.experimental import pallas as pl
from jax.experimental.pallas import tpu as pltpu
from jax.sharding import PartitionSpec as P

AGE = 128
DT = 4
ITERS = 4
LANES = 128
WIN = DT + 3
MXU = 256
STEP = 8
SHARE = 4
ROWS = 2 * WIN * 16
CHUNKS = 4
LISTS = 4
VMEM_SPREAD = 67043328


f32 = jnp.float32
bf16 = jnp.bfloat16


def spline(frac):
    rest = 1.0 - frac
    cube = frac * frac * frac
    return (
        rest * rest * rest / 6.0,
        (3.0 * cube - 6.0 * frac * frac + 4.0) / 6.0,
        (-3.0 * cube + 3.0 * frac * frac + 3.0 * frac + 1.0) / 6.0,
        cube / 6.0,
    )


def spread_body(
    blocks,
    tiles,
    core_ref,
    tile_ref,
    age_hbm,
    off_hbm,
    code_hbm,
    age_frac_hbm,
    dur_frac_hbm,
    expo_hbm,
    claim_hbm,
    keep_ref,
    send_ref,
    age_ref,
    off_ref,
    code_ref,
    age_frac_ref,
    dur_frac_ref,
    expo_ref,
    claim_ref,
    base_s,
    group_s,
    code_s,
    weight_s,
    term_s,
    acc_s,
    order_s,
    steps_s,
    *places_and_sems,
):
    at, sems = places_and_sems[:LISTS], places_and_sems[LISTS]
    slab = 8
    dur = tiles * DT
    part = blocks // CHUNKS
    quarter = blocks // LISTS
    sources = (age_hbm, off_hbm, code_hbm, age_frac_hbm, dur_frac_hbm, expo_hbm, claim_hbm)
    targets = (age_ref, off_ref, code_ref, age_frac_ref, dur_frac_ref, expo_ref, claim_ref)
    copies = []
    for c in range(CHUNKS):
        rows = pl.ds(c * part, part)
        copies.append(
            [
                pltpu.make_async_copy(source.at[rows], target.at[rows], sems.at[c, k])
                for k, (source, target) in enumerate(zip(sources, targets))
            ]
        )
        for copy in copies[-1]:
            copy.start()

    def clear(t, _):
        for place in at:
            place[t] = 0
        return 0

    lax.fori_loop(0, tiles, clear, 0)

    def tally(i, _):
        for j in range(2):
            for k, place in enumerate(at):
                t = tile_ref[k * quarter + i * 2 + j]
                place[t] = place[t] + 1
        return 0

    lax.fori_loop(0, quarter // 2, tally, 0)

    def starts(t, start):
        end = start
        for place in at:
            count = place[t]
            place[t] = end
            end = end + count
        for j in range(STEP - 1):
            order_s[end + j] = blocks
        steps = lax.div(end - start + (STEP - 1), STEP)
        steps_s[t] = steps
        return start + steps * STEP

    padded = lax.fori_loop(0, tiles, starts, jnp.int32(0))
    for j in range(STEP // 2):
        order_s[padded + j] = blocks

    acc_s[...] = jnp.zeros_like(acc_s)
    blank = jnp.zeros((slab, LANES), f32)
    pad = pl.ds(blocks, slab)
    base_s[pad] = blank
    group_s[pad] = blank
    code_s[pad] = blank - 1.0
    for place in range(4):
        weight_s[place, pad] = blank
    for row in range(2 * WIN):
        term_s[row, pad] = blank

    def prepare(i, _):
        rows = pl.ds(pl.multiple_of(i * slab, slab), slab)
        first = age_ref[rows] - 1
        base_s[rows] = (first & 15).astype(f32)
        group_s[rows] = (first >> 4).astype(f32)
        code_s[rows] = code_ref[rows].astype(f32)
        for place, weight in enumerate(spline(age_frac_ref[rows])):
            weight_s[place, rows] = weight.astype(bf16).astype(f32)
        dur_w = spline(dur_frac_ref[rows])
        offset = off_ref[rows]
        is_offset = [offset == o for o in range(DT)]
        for channel, value in enumerate((expo_ref[rows], claim_ref[rows])):
            terms = [(w * value).astype(bf16).astype(f32) for w in dur_w]
            for cell in range(WIN):
                term = jnp.zeros((slab, LANES), f32)
                for o in range(DT):
                    if 0 <= cell - o < 4:
                        term = jnp.where(is_offset[o], terms[cell - o], term)
                term_s[channel * WIN + cell, rows] = term
        for j in range(2):
            for k, place in enumerate(at):
                block = k * quarter + i * 2 + j
                t = tile_ref[block]
                spot = place[t]
                order_s[spot] = block
                place[t] = spot + 1
        return 0

    for c in range(CHUNKS):
        for copy in copies[c]:
            copy.wait()
        lax.fori_loop(c * (part // slab), (c + 1) * (part // slab), prepare, 0)

    row16 = lax.broadcasted_iota(jnp.int32, (16, LANES), 0)
    row16b = row16.astype(f32).astype(bf16)
    codes = [(half * 8 + (row16 & 7)).astype(f32).astype(bf16) for half in range(2)]
    zero = jnp.zeros((16, LANES), bf16)

    def spread_row(ref, r, count=16):
        return jnp.broadcast_to(ref[pl.ds(r, 1), :], (count, LANES))

    def build(r, left_ref, ages_ref):
        base = spread_row(base_s, r).astype(bf16)
        group = spread_row(group_s, r).astype(bf16)
        weights = [spread_row(weight_s.at[place], r).astype(bf16) for place in range(4)]
        ahead = row16b - base
        wraps = ahead < 0
        place = jnp.where(wraps, ahead + 16, ahead)
        pattern = zero
        for k in range(4):
            pattern = jnp.where(place == k, weights[k], pattern)
        owner = jnp.where(wraps, group + 1, group)
        for a in range(AGE // 16):
            ages_ref[a] = jnp.where(owner == a, pattern, zero)
        code = spread_row(code_s, r).astype(bf16)
        masks = [code == c for c in codes]
        for cell in range(WIN):
            expo = spread_row(term_s.at[cell], r, 8)
            claim = spread_row(term_s.at[WIN + cell], r, 8)
            both = jnp.concatenate([expo, claim], axis=0).astype(bf16)
            for half in range(2):
                left_ref[half * WIN + cell] = jnp.where(masks[half], both, zero)

    def fill(first, left, ages):
        for j in range(STEP // 2):
            build(order_s[first + j], left.at[j], ages.at[j])

    def all_tiles(left_a, left_b, ages_a, ages_b, acc0, acc1):
        for left in (left_a, left_b):
            left[:, ROWS // 16 :] = jnp.zeros((STEP // 2, (MXU - ROWS) // 16, 16, LANES), bf16)
        fill(0, left_a, ages_a)

        def multiply(left, ages, stage):
            for unit, acc in enumerate((acc0, acc1)):
                pair = (2 * unit, 2 * unit + 1)
                pltpu.matmul_push_rhs(
                    jnp.concatenate([left[j].reshape(MXU, LANES) for j in pair], axis=1),
                    stage,
                    unit,
                    transpose=True,
                )
                pltpu.matmul_acc_lhs(
                    acc,
                    jnp.concatenate([ages[j].reshape(AGE, LANES) for j in pair], axis=1),
                    load_staged_rhs=stage,
                )

        def one_tile(t, done):
            steps = steps_s[t]

            def step(s, _):
                first = (done + s) * STEP
                fill(first + STEP // 2, left_b, ages_b)
                multiply(left_a, ages_a, 0)
                fill(first + STEP, left_a, ages_a)
                multiply(left_b, ages_b, 1)
                return 0

            @pl.when(steps > 0)
            def _():
                lax.fori_loop(0, steps, step, 0)
                total = (pltpu.matmul_pop(acc0) + pltpu.matmul_pop(acc1)).T
                total = total[:ROWS].reshape(2, WIN, 2, 8, LANES)
                for half in range(2):
                    for cell in range(WIN):
                        for channel in range(2):
                            acc_s[half * 2 + channel, t * DT + cell] += total[half, cell, channel]

            return done + steps

        lax.fori_loop(0, tiles, one_tile, jnp.int32(0))

    pl.run_scoped(
        all_tiles,
        *[pltpu.VMEM((STEP // 2, MXU // 16, 16, LANES), bf16)] * 2,
        *[pltpu.VMEM((STEP // 2, AGE // 16, 16, LANES), bf16)] * 2,
        pltpu.ACC(0)((AGE, MXU), f32),
        pltpu.ACC(1)((AGE, MXU), f32),
    )

    low = lax.broadcasted_iota(jnp.int32, (8, LANES), 0) < 4
    mine = core_ref[0]
    for whose, half in enumerate((mine, 1 - mine)):
        expo = acc_s[half * 2, 1 : dur + 1]
        claim = acc_s[half * 2 + 1, 1 : dur + 1]
        quarters = (
            jnp.where(low, expo, pltpu.roll(claim, 4, 1)),
            jnp.where(low, pltpu.roll(expo, 4, 1), claim),
        )
        for q in range(2):
            if whose == 0:
                keep_ref[q] = quarters[q]
            else:
                send_ref[pl.ds(q * dur, dur)] = quarters[q]
    for channel in range(2):
        pooled = jnp.sum(
            acc_s[channel, 1 : dur + 1] + acc_s[2 + channel, 1 : dur + 1], axis=1
        )
        base = 2 * dur + channel * (dur // 8)
        send_ref[pl.ds(base, dur // 8)] = pooled.reshape(dur // 8, 8, LANES)


def spread(core, tile_ids, fields, tiles):
    blocks = tile_ids.shape[0]
    assert blocks % (8 * CHUNKS) == 0
    dur = tiles * DT
    rows = blocks + 8
    vmem = pl.BlockSpec(memory_space=pltpu.VMEM)
    smem = pl.BlockSpec(memory_space=pltpu.SMEM)
    hbm = pl.BlockSpec(memory_space=pltpu.HBM)
    return pl.pallas_call(
        functools.partial(spread_body, blocks, tiles),
        out_shape=(
            jax.ShapeDtypeStruct((2, dur, 8, LANES), f32),
            jax.ShapeDtypeStruct((2 * dur + 2 * (dur // 8), 8, LANES), f32),
        ),
        in_specs=[smem, smem] + [hbm] * 7,
        out_specs=(vmem, vmem),
        scratch_shapes=[
            *[pltpu.VMEM((blocks, LANES), jnp.int32)] * 3,
            *[pltpu.VMEM((blocks, LANES), f32)] * 4,
            pltpu.VMEM((rows, LANES), f32),
            pltpu.VMEM((rows, LANES), f32),
            pltpu.VMEM((rows, LANES), f32),
            pltpu.VMEM((4, rows, LANES), f32),
            pltpu.VMEM((2 * WIN, rows, LANES), f32),
            pltpu.VMEM((4, dur + 3, 8, LANES), f32),
            pltpu.SMEM((blocks + STEP * tiles + 2 * STEP,), jnp.int32),
            *[pltpu.SMEM((tiles,), jnp.int32)] * (LISTS + 1),
            pltpu.SemaphoreType.DMA((CHUNKS, 7)),
        ],
        compiler_params=pltpu.CompilerParams(vmem_limit_bytes=VMEM_SPREAD),
        name="spread",
    )(core, tile_ids, *fields)


def smooth_body(
    dur,
    where_ref,
    age_w_ref,
    dur_w_ref,
    cred_ref,
    grid_a_ref,
    grid_b_ref,
    pool_a_ref,
    pool_b_ref,
    out_ref,
    prior_s,
    x_s,
    r_s,
):
    half = dur // 2
    slot, high = where_ref[0], where_ref[1]
    sub = lax.broadcasted_iota(jnp.int32, (8, LANES), 0)
    lane = lax.broadcasted_iota(jnp.int32, (1, 8, LANES), 2)
    low = sub < 4

    def swap(v):
        return pltpu.roll(v, 4, v.ndim - 2)

    def per_transition(ref):
        value = jnp.full((8, LANES), ref[slot], f32)
        for t in range(1, 4):
            value = jnp.where((sub & 3) == t, ref[slot + t], value)
        return value

    weight_a, weight_d, cred = map(per_transition, (age_w_ref, dur_w_ref, cred_ref))
    pool = pool_a_ref[...] + pool_b_ref[...]
    eighth = dur // 8
    prior_s[...] = (pool[eighth:] / (1.0 + pool[:eighth])).reshape(dur, LANES)
    grid = grid_a_ref[...] + grid_b_ref[...]
    top, bottom = grid[:half], grid[half:]
    diagonal = jnp.where(low, top, swap(bottom)) + cred
    claims = jnp.where(low, swap(top), bottom)
    prior = jnp.stack(
        [
            jnp.where(
                low,
                jnp.broadcast_to(prior_s[pl.ds(d, 1), :], (8, LANES)),
                jnp.broadcast_to(prior_s[pl.ds(half + d, 1), :], (8, LANES)),
            )
            for d in range(half)
        ]
    )
    rhs = claims + cred * prior

    def operate(v):
        y = v - 2.0 * pltpu.roll(v, LANES - 1, 2) + pltpu.roll(v, LANES - 2, 2)
        y = jnp.where(lane < AGE - 2, y, 0.0)
        along_age = y - 2.0 * pltpu.roll(y, 1, 2) + pltpu.roll(y, 2, 2)
        longer = jnp.concatenate([v, swap(v[:2])], axis=0)
        y = longer[:half] - 2.0 * longer[1 : half + 1] + longer[2 : half + 2]
        y = jnp.concatenate([y[: half - 2], jnp.where(low, y[half - 2 :], 0.0)], axis=0)
        longer = jnp.concatenate([jnp.where(low, 0.0, swap(y[half - 2 :])), y], axis=0)
        along_dur = longer[2:] - 2.0 * longer[1 : half + 1] + longer[:half]
        return diagonal * v + weight_a * along_age + weight_d * along_dur

    def inner(a, b):
        part = jnp.sum(a * b, axis=0)
        part = part + swap(part)
        return jnp.sum(part, axis=1, keepdims=True)

    x = jnp.zeros_like(rhs)
    r = rhs
    p = rhs
    norm = inner(r, r)
    for turn in range(ITERS):
        image = operate(p)
        alpha = norm / inner(p, image)
        x = x + alpha * p
        r = r - alpha * image
        if turn < ITERS - 1:
            after = inner(r, r)
            p = r + (after / norm) * p
            norm = after
    x_s[...] = x
    r_s[...] = r
    span = SHARE * DT
    in_low = high * span < half
    start = jnp.where(in_low, high * span, high * span - half)
    for dest in range(SHARE):
        for d in range(DT):
            xv = x_s[start + dest * DT + d]
            rv = r_s[start + dest * DT + d]
            row = jnp.where(
                in_low, jnp.where(low, xv, swap(rv)), jnp.where(low, swap(xv), rv)
            )
            out_ref[dest, pl.ds(d, 8, stride=DT), :] = row


def smooth(where, weights, grid_a, grid_b, pool_a, pool_b):
    dur = grid_a.shape[0]
    vmem = pl.BlockSpec(memory_space=pltpu.VMEM)
    smem = pl.BlockSpec(memory_space=pltpu.SMEM)
    return pl.pallas_call(
        functools.partial(smooth_body, dur),
        out_shape=jax.ShapeDtypeStruct((SHARE, 8 * DT, LANES), f32),
        in_specs=[smem] * 4 + [vmem] * 4,
        out_specs=vmem,
        scratch_shapes=[
            pltpu.VMEM((dur, LANES), f32),
            pltpu.VMEM((dur // 2, 8, LANES), f32),
            pltpu.VMEM((dur // 2, 8, LANES), f32),
        ],
        compiler_params=pltpu.CompilerParams(vmem_limit_bytes=32 * 1024 * 1024),
        name="smooth",
    )(where, *weights, grid_a, grid_b, pool_a, pool_b)


def gather_body(me_ref, own_ref, one_ref, two_ref, three_ref, x_ref, r_ref):
    me = me_ref[0]
    for k, ref in enumerate((own_ref, one_ref, two_ref, three_ref)):
        other = me ^ k
        slot = (other & 1) * 2 + (other >> 1)
        got = ref[me] if k == 0 else ref[...]
        x_ref[slot] = got[: 4 * DT]
        r_ref[slot] = got[4 * DT :]


def gather(me, own, others):
    vmem = pl.BlockSpec(memory_space=pltpu.VMEM)
    smem = pl.BlockSpec(memory_space=pltpu.SMEM)
    shape = jax.ShapeDtypeStruct((SHARE, 4 * DT, LANES), f32)
    return pl.pallas_call(
        gather_body,
        out_shape=(shape, shape),
        in_specs=[smem] + [vmem] * 4,
        out_specs=(vmem, vmem),
        compiler_params=pltpu.CompilerParams(vmem_limit_bytes=4 * 1024 * 1024),
        name="gather",
    )(me, own, *others)


def swap_with(value, axis, bit):
    size = lax.axis_size(axis)
    return lax.ppermute(value, axis, [(i, i ^ bit) for i in range(size)])


def bits_of(size):
    bits = [1 << k for k in range(size.bit_length() - 1)]
    assert 1 << len(bits) == size, size
    return bits


def per_device(
    age_cell,
    dur_cell,
    trans_code,
    age_frac,
    dur_frac,
    exposure,
    claims,
    block_tile,
    smooth_age,
    smooth_dur,
    credibility,
):
    trans_dev = smooth_age.shape[0]
    tiles = lax.axis_size("tile")
    groups = lax.axis_size("tg")
    dur = tiles * DT
    assert trans_dev == 4 * SHARE and tiles % 8 == 0
    here = lax.axis_index("tile")
    core, near, high = here & 1, (here >> 1) & 1, here >> 2
    tile_ids = block_tile.reshape(-1)
    blocks = tile_ids.shape[0]
    fields = [
        field.reshape(blocks, LANES)
        for field in (age_cell, dur_cell, trans_code, age_frac, dur_frac, exposure, claims)
    ]
    keep, send = spread(core.reshape(1), tile_ids, fields, tiles)
    got = swap_with(send, "tile", 1)
    pool = send[2 * dur :] + got[2 * dur :]
    got = got[: 2 * dur].reshape(keep.shape)

    def quarter(at):
        return lax.dynamic_index_in_dim(keep, at, 0, False) + lax.dynamic_index_in_dim(
            got, at, 0, False
        )

    grid = quarter(near) + swap_with(quarter(1 - near), "tile", 2)
    tile_bits = bits_of(tiles)
    pool_bits = [("tg", bit) for bit in bits_of(groups)] + [("tile", bit) for bit in tile_bits[1:]]
    for axis, bit in pool_bits[:-1]:
        pool = pool + swap_with(pool, axis, bit)
    pool_other = swap_with(pool, *pool_bits[-1])
    for bit in tile_bits[2:-1]:
        grid = grid + swap_with(grid, "tile", bit)
    grid_other = swap_with(grid, "tile", tile_bits[-1])
    slot = core * 8 + near * 4
    own = smooth(
        jnp.stack([slot, high]),
        (smooth_age, smooth_dur, credibility),
        grid,
        grid_other,
        pool,
        pool_other,
    )
    me = here & 3
    others = [
        swap_with(lax.dynamic_index_in_dim(own, me ^ k, 0, False), "tile", k) for k in (1, 2, 3)
    ]
    smoothed, residual = gather(me.reshape(1), own, others)
    shape = (trans_dev, DT, AGE)
    return smoothed.reshape(shape), residual.reshape(shape)


def solution(mesh):
    records = P("tg", "tile")
    in_specs = (records,) * 7 + (P("tg", "tile", None),) + (P("tg"),) * 3
    out_specs = (P("tg", "tile", None), P("tg", "tile", None))
    mapped = jax.shard_map(
        per_device, mesh=mesh, in_specs=in_specs, out_specs=out_specs, check_vma=False
    )

    def run(*args):
        with jax.sharding.use_abstract_mesh(mesh.abstract_mesh):
            return mapped(*args)

    return run
```

```python
import functools

import jax
import jax.numpy as jnp
from jax import lax
from jax.experimental import pallas as pl
from jax.experimental.pallas import tpu as pltpu
from jax.sharding import PartitionSpec as P

AGE = 128
DT = 4
ITERS = 4
LANES = 128
WIN = DT + 3
MXU = 256
STEP = 8
SHARE = 4
ROWS = 2 * WIN * 16
CHUNKS = 4
LISTS = 4
VMEM_SPREAD = 67043328


f32 = jnp.float32
bf16 = jnp.bfloat16


def spline(frac):
    rest = 1.0 - frac
    cube = frac * frac * frac
    return (
        rest * rest * rest / 6.0,
        (3.0 * cube - 6.0 * frac * frac + 4.0) / 6.0,
        (-3.0 * cube + 3.0 * frac * frac + 3.0 * frac + 1.0) / 6.0,
        cube / 6.0,
    )


def spread_body(
    blocks,
    tiles,
    core_ref,
    tile_ref,
    age_hbm,
    off_hbm,
    code_hbm,
    age_frac_hbm,
    dur_frac_hbm,
    expo_hbm,
    claim_hbm,
    keep_ref,
    send_ref,
    age_ref,
    off_ref,
    code_ref,
    age_frac_ref,
    dur_frac_ref,
    expo_ref,
    claim_ref,
    base_s,
    group_s,
    code_s,
    weight_s,
    term_s,
    acc_s,
    order_s,
    steps_s,
    *places_and_sems,
):
    at, sems = places_and_sems[:LISTS], places_and_sems[LISTS]
    slab = 8
    dur = tiles * DT
    part = blocks // CHUNKS
    quarter = blocks // LISTS
    sources = (age_hbm, off_hbm, code_hbm, age_frac_hbm, dur_frac_hbm, expo_hbm, claim_hbm)
    targets = (age_ref, off_ref, code_ref, age_frac_ref, dur_frac_ref, expo_ref, claim_ref)
    copies = []
    for c in range(CHUNKS):
        rows = pl.ds(c * part, part)
        copies.append(
            [
                pltpu.make_async_copy(source.at[rows], target.at[rows], sems.at[c, k])
                for k, (source, target) in enumerate(zip(sources, targets))
            ]
        )
        for copy in copies[-1]:
            copy.start()

    def clear(t, _):
        for place in at:
            place[t] = 0
        return 0

    lax.fori_loop(0, tiles, clear, 0)

    def tally(i, _):
        for j in range(2):
            for k, place in enumerate(at):
                t = tile_ref[k * quarter + i * 2 + j]
                place[t] = place[t] + 1
        return 0

    lax.fori_loop(0, quarter // 2, tally, 0)

    def starts(t, start):
        end = start
        for place in at:
            count = place[t]
            place[t] = end
            end = end + count
        for j in range(STEP - 1):
            order_s[end + j] = blocks
        steps = lax.div(end - start + (STEP - 1), STEP)
        steps_s[t] = steps
        return start + steps * STEP

    padded = lax.fori_loop(0, tiles, starts, jnp.int32(0))
    for j in range(STEP):
        order_s[padded + j] = blocks

    acc_s[...] = jnp.zeros_like(acc_s)
    blank = jnp.zeros((slab, LANES), f32)
    pad = pl.ds(blocks, slab)
    base_s[pad] = blank
    group_s[pad] = blank
    code_s[pad] = blank - 1.0
    for place in range(4):
        weight_s[place, pad] = blank
    for row in range(2 * WIN):
        term_s[row, pad] = blank

    def prepare(i, _):
        rows = pl.ds(pl.multiple_of(i * slab, slab), slab)
        first = age_ref[rows] - 1
        base_s[rows] = (first & 15).astype(f32)
        group_s[rows] = (first >> 4).astype(f32)
        code_s[rows] = code_ref[rows].astype(f32)
        for place, weight in enumerate(spline(age_frac_ref[rows])):
            weight_s[place, rows] = weight.astype(bf16).astype(f32)
        dur_w = spline(dur_frac_ref[rows])
        offset = off_ref[rows]
        is_offset = [offset == o for o in range(DT)]
        for channel, value in enumerate((expo_ref[rows], claim_ref[rows])):
            terms = [(w * value).astype(bf16).astype(f32) for w in dur_w]
            for cell in range(WIN):
                term = jnp.zeros((slab, LANES), f32)
                for o in range(DT):
                    if 0 <= cell - o < 4:
                        term = jnp.where(is_offset[o], terms[cell - o], term)
                term_s[channel * WIN + cell, rows] = term
        for j in range(2):
            for k, place in enumerate(at):
                block = k * quarter + i * 2 + j
                t = tile_ref[block]
                spot = place[t]
                order_s[spot] = block
                place[t] = spot + 1
        return 0

    for c in range(CHUNKS):
        for copy in copies[c]:
            copy.wait()
        lax.fori_loop(c * (part // slab), (c + 1) * (part // slab), prepare, 0)

    row16 = lax.broadcasted_iota(jnp.int32, (16, LANES), 0)
    row16b = row16.astype(f32).astype(bf16)
    codes = [(half * 8 + (row16 & 7)).astype(f32).astype(bf16) for half in range(2)]
    zero = jnp.zeros((16, LANES), bf16)

    def spread_row(ref, r, count=16):
        return jnp.broadcast_to(ref[pl.ds(r, 1), :], (count, LANES))

    def build(r, left_ref):
        base = spread_row(base_s, r).astype(bf16)
        group = spread_row(group_s, r).astype(bf16)
        weights = [spread_row(weight_s.at[place], r).astype(bf16) for place in range(4)]
        ahead = row16b - base
        wraps = ahead < 0
        place = jnp.where(wraps, ahead + 16, ahead)
        pattern = zero
        for k in range(4):
            pattern = jnp.where(place == k, weights[k], pattern)
        owner = jnp.where(wraps, group + 1, group)
        code = spread_row(code_s, r).astype(bf16)
        masks = [code == c for c in codes]
        for cell in range(WIN):
            expo = spread_row(term_s.at[cell], r, 8)
            claim = spread_row(term_s.at[WIN + cell], r, 8)
            both = jnp.concatenate([expo, claim], axis=0).astype(bf16)
            for half in range(2):
                left_ref[half * WIN + cell] = jnp.where(masks[half], both, zero)
        return jnp.concatenate(
            [jnp.where(owner == a, pattern, zero) for a in range(AGE // 16)], axis=0
        )

    def all_tiles(left_a, left_b, *accs):
        def fill(first, left, stage):
            for unit in range(2):
                ages = [
                    build(order_s[first + 4 * unit + j], left.at[4 * unit + j]) for j in range(4)
                ]
                pairs = [jnp.concatenate(ages[j : j + 2], axis=1) for j in (0, 2)]
                pltpu.matmul_push_rhs(
                    jnp.concatenate(pairs, axis=0), stage, unit, transpose=True
                )

        def multiply(left, stage):
            for pair in range(2):
                for unit in range(2):
                    j = 4 * unit + 2 * pair
                    rows = [left[j + k].reshape(ROWS, LANES) for k in range(2)]
                    pltpu.matmul_acc_lhs(
                        accs[2 * unit + pair],
                        jnp.concatenate(rows, axis=1),
                        load_staged_rhs=stage if pair == 0 else None,
                    )

        def take():
            totals = [pltpu.matmul_pop(acc) for acc in accs]
            return (totals[0][:, :AGE] + totals[1][:, AGE:]) + (
                totals[2][:, :AGE] + totals[3][:, AGE:]
            )

        fill(0, left_a, 0)

        def one_tile(t, done):
            steps = steps_s[t]
            odd = steps & 1

            @pl.when(steps > 0)
            def _():
                @pl.when(odd == 1)
                def _():
                    multiply(left_a, 0)
                    fill((done + 1) * STEP, left_a, 0)

                def two_steps(s, _):
                    first = (done + odd + 2 * s) * STEP
                    fill(first + STEP, left_b, 1)
                    multiply(left_a, 0)
                    fill(first + 2 * STEP, left_a, 0)
                    multiply(left_b, 1)
                    return 0

                lax.fori_loop(0, steps >> 1, two_steps, 0)
                total = take().reshape(2, WIN, 2, 8, LANES)
                for half in range(2):
                    for cell in range(WIN):
                        for channel in range(2):
                            acc_s[half * 2 + channel, t * DT + cell] += total[half, cell, channel]

            return done + steps

        lax.fori_loop(0, tiles, one_tile, jnp.int32(0))
        multiply(left_a, 0)
        acc_s[0, 0] = take()[:8]

    pl.run_scoped(
        all_tiles,
        *[pltpu.VMEM((STEP, ROWS // 16, 16, LANES), bf16)] * 2,
        *[pltpu.ACC(unit)((ROWS, MXU), f32) for unit in (0, 0, 1, 1)],
    )

    low = lax.broadcasted_iota(jnp.int32, (8, LANES), 0) < 4
    mine = core_ref[0]
    for whose, half in enumerate((mine, 1 - mine)):
        expo = acc_s[half * 2, 1 : dur + 1]
        claim = acc_s[half * 2 + 1, 1 : dur + 1]
        quarters = (
            jnp.where(low, expo, pltpu.roll(claim, 4, 1)),
            jnp.where(low, pltpu.roll(expo, 4, 1), claim),
        )
        for q in range(2):
            if whose == 0:
                keep_ref[q] = quarters[q]
            else:
                send_ref[pl.ds(q * dur, dur)] = quarters[q]
    for channel in range(2):
        pooled = jnp.sum(
            acc_s[channel, 1 : dur + 1] + acc_s[2 + channel, 1 : dur + 1], axis=1
        )
        base = 2 * dur + channel * (dur // 8)
        send_ref[pl.ds(base, dur // 8)] = pooled.reshape(dur // 8, 8, LANES)


def spread(core, tile_ids, fields, tiles):
    blocks = tile_ids.shape[0]
    assert blocks % (8 * CHUNKS) == 0
    dur = tiles * DT
    rows = blocks + 8
    vmem = pl.BlockSpec(memory_space=pltpu.VMEM)
    smem = pl.BlockSpec(memory_space=pltpu.SMEM)
    hbm = pl.BlockSpec(memory_space=pltpu.HBM)
    return pl.pallas_call(
        functools.partial(spread_body, blocks, tiles),
        out_shape=(
            jax.ShapeDtypeStruct((2, dur, 8, LANES), f32),
            jax.ShapeDtypeStruct((2 * dur + 2 * (dur // 8), 8, LANES), f32),
        ),
        in_specs=[smem, smem] + [hbm] * 7,
        out_specs=(vmem, vmem),
        scratch_shapes=[
            *[pltpu.VMEM((blocks, LANES), jnp.int32)] * 3,
            *[pltpu.VMEM((blocks, LANES), f32)] * 4,
            pltpu.VMEM((rows, LANES), f32),
            pltpu.VMEM((rows, LANES), f32),
            pltpu.VMEM((rows, LANES), f32),
            pltpu.VMEM((4, rows, LANES), f32),
            pltpu.VMEM((2 * WIN, rows, LANES), f32),
            pltpu.VMEM((4, dur + 3, 8, LANES), f32),
            pltpu.SMEM((blocks + STEP * tiles + 2 * STEP,), jnp.int32),
            *[pltpu.SMEM((tiles,), jnp.int32)] * (LISTS + 1),
            pltpu.SemaphoreType.DMA((CHUNKS, 7)),
        ],
        compiler_params=pltpu.CompilerParams(vmem_limit_bytes=VMEM_SPREAD),
        name="spread",
    )(core, tile_ids, *fields)


def smooth_body(
    dur,
    where_ref,
    age_w_ref,
    dur_w_ref,
    cred_ref,
    grid_a_ref,
    grid_b_ref,
    pool_a_ref,
    pool_b_ref,
    out_ref,
    prior_s,
    x_s,
    r_s,
):
    half = dur // 2
    slot, high = where_ref[0], where_ref[1]
    sub = lax.broadcasted_iota(jnp.int32, (8, LANES), 0)
    lane = lax.broadcasted_iota(jnp.int32, (1, 8, LANES), 2)
    low = sub < 4

    def swap(v):
        return pltpu.roll(v, 4, v.ndim - 2)

    def per_transition(ref):
        value = jnp.full((8, LANES), ref[slot], f32)
        for t in range(1, 4):
            value = jnp.where((sub & 3) == t, ref[slot + t], value)
        return value

    weight_a, weight_d, cred = map(per_transition, (age_w_ref, dur_w_ref, cred_ref))
    pool = pool_a_ref[...] + pool_b_ref[...]
    eighth = dur // 8
    prior_s[...] = (pool[eighth:] / (1.0 + pool[:eighth])).reshape(dur, LANES)
    grid = grid_a_ref[...] + grid_b_ref[...]
    top, bottom = grid[:half], grid[half:]
    diagonal = jnp.where(low, top, swap(bottom)) + cred
    claims = jnp.where(low, swap(top), bottom)
    prior = jnp.stack(
        [
            jnp.where(
                low,
                jnp.broadcast_to(prior_s[pl.ds(d, 1), :], (8, LANES)),
                jnp.broadcast_to(prior_s[pl.ds(half + d, 1), :], (8, LANES)),
            )
            for d in range(half)
        ]
    )
    rhs = claims + cred * prior

    def operate(v):
        y = v - 2.0 * pltpu.roll(v, LANES - 1, 2) + pltpu.roll(v, LANES - 2, 2)
        y = jnp.where(lane < AGE - 2, y, 0.0)
        along_age = y - 2.0 * pltpu.roll(y, 1, 2) + pltpu.roll(y, 2, 2)
        longer = jnp.concatenate([v, swap(v[:2])], axis=0)
        y = longer[:half] - 2.0 * longer[1 : half + 1] + longer[2 : half + 2]
        y = jnp.concatenate([y[: half - 2], jnp.where(low, y[half - 2 :], 0.0)], axis=0)
        longer = jnp.concatenate([jnp.where(low, 0.0, swap(y[half - 2 :])), y], axis=0)
        along_dur = longer[2:] - 2.0 * longer[1 : half + 1] + longer[:half]
        return diagonal * v + weight_a * along_age + weight_d * along_dur

    def inner(a, b):
        part = jnp.sum(a * b, axis=0)
        part = part + swap(part)
        return jnp.sum(part, axis=1, keepdims=True)

    x = jnp.zeros_like(rhs)
    r = rhs
    p = rhs
    norm = inner(r, r)
    for turn in range(ITERS):
        image = operate(p)
        alpha = norm / inner(p, image)
        x = x + alpha * p
        r = r - alpha * image
        if turn < ITERS - 1:
            after = inner(r, r)
            p = r + (after / norm) * p
            norm = after
    x_s[...] = x
    r_s[...] = r
    span = SHARE * DT
    in_low = high * span < half
    start = jnp.where(in_low, high * span, high * span - half)
    for dest in range(SHARE):
        for d in range(DT):
            xv = x_s[start + dest * DT + d]
            rv = r_s[start + dest * DT + d]
            row = jnp.where(
                in_low, jnp.where(low, xv, swap(rv)), jnp.where(low, swap(xv), rv)
            )
            out_ref[dest, pl.ds(d, 8, stride=DT), :] = row


def smooth(where, weights, grid_a, grid_b, pool_a, pool_b):
    dur = grid_a.shape[0]
    vmem = pl.BlockSpec(memory_space=pltpu.VMEM)
    smem = pl.BlockSpec(memory_space=pltpu.SMEM)
    return pl.pallas_call(
        functools.partial(smooth_body, dur),
        out_shape=jax.ShapeDtypeStruct((SHARE, 8 * DT, LANES), f32),
        in_specs=[smem] * 4 + [vmem] * 4,
        out_specs=vmem,
        scratch_shapes=[
            pltpu.VMEM((dur, LANES), f32),
            pltpu.VMEM((dur // 2, 8, LANES), f32),
            pltpu.VMEM((dur // 2, 8, LANES), f32),
        ],
        compiler_params=pltpu.CompilerParams(vmem_limit_bytes=32 * 1024 * 1024),
        name="smooth",
    )(where, *weights, grid_a, grid_b, pool_a, pool_b)


def gather_body(me_ref, own_ref, one_ref, two_ref, three_ref, x_ref, r_ref):
    me = me_ref[0]
    for k, ref in enumerate((own_ref, one_ref, two_ref, three_ref)):
        other = me ^ k
        slot = (other & 1) * 2 + (other >> 1)
        got = ref[me] if k == 0 else ref[...]
        x_ref[slot] = got[: 4 * DT]
        r_ref[slot] = got[4 * DT :]


def gather(me, own, others):
    vmem = pl.BlockSpec(memory_space=pltpu.VMEM)
    smem = pl.BlockSpec(memory_space=pltpu.SMEM)
    shape = jax.ShapeDtypeStruct((SHARE, 4 * DT, LANES), f32)
    return pl.pallas_call(
        gather_body,
        out_shape=(shape, shape),
        in_specs=[smem] + [vmem] * 4,
        out_specs=(vmem, vmem),
        compiler_params=pltpu.CompilerParams(vmem_limit_bytes=4 * 1024 * 1024),
        name="gather",
    )(me, own, *others)


def swap_with(value, axis, bit):
    size = lax.axis_size(axis)
    return lax.ppermute(value, axis, [(i, i ^ bit) for i in range(size)])


def bits_of(size):
    bits = [1 << k for k in range(size.bit_length() - 1)]
    assert 1 << len(bits) == size, size
    return bits


def per_device(
    age_cell,
    dur_cell,
    trans_code,
    age_frac,
    dur_frac,
    exposure,
    claims,
    block_tile,
    smooth_age,
    smooth_dur,
    credibility,
):
    trans_dev = smooth_age.shape[0]
    tiles = lax.axis_size("tile")
    groups = lax.axis_size("tg")
    dur = tiles * DT
    assert trans_dev == 4 * SHARE and tiles % 8 == 0
    here = lax.axis_index("tile")
    core, near, high = here & 1, (here >> 1) & 1, here >> 2
    tile_ids = block_tile.reshape(-1)
    blocks = tile_ids.shape[0]
    fields = [
        field.reshape(blocks, LANES)
        for field in (age_cell, dur_cell, trans_code, age_frac, dur_frac, exposure, claims)
    ]
    keep, send = spread(core.reshape(1), tile_ids, fields, tiles)
    got = swap_with(send, "tile", 1)
    pool = send[2 * dur :] + got[2 * dur :]
    got = got[: 2 * dur].reshape(keep.shape)

    def quarter(at):
        return lax.dynamic_index_in_dim(keep, at, 0, False) + lax.dynamic_index_in_dim(
            got, at, 0, False
        )

    grid = quarter(near) + swap_with(quarter(1 - near), "tile", 2)
    tile_bits = bits_of(tiles)
    pool_bits = [("tg", bit) for bit in bits_of(groups)] + [("tile", bit) for bit in tile_bits[1:]]
    for axis, bit in pool_bits[:-1]:
        pool = pool + swap_with(pool, axis, bit)
    pool_other = swap_with(pool, *pool_bits[-1])
    for bit in tile_bits[2:-1]:
        grid = grid + swap_with(grid, "tile", bit)
    grid_other = swap_with(grid, "tile", tile_bits[-1])
    slot = core * 8 + near * 4
    own = smooth(
        jnp.stack([slot, high]),
        (smooth_age, smooth_dur, credibility),
        grid,
        grid_other,
        pool,
        pool_other,
    )
    me = here & 3
    others = [
        swap_with(lax.dynamic_index_in_dim(own, me ^ k, 0, False), "tile", k) for k in (1, 2, 3)
    ]
    smoothed, residual = gather(me.reshape(1), own, others)
    shape = (trans_dev, DT, AGE)
    return smoothed.reshape(shape), residual.reshape(shape)


def solution(mesh):
    records = P("tg", "tile")
    in_specs = (records,) * 7 + (P("tg", "tile", None),) + (P("tg"),) * 3
    out_specs = (P("tg", "tile", None), P("tg", "tile", None))
    mapped = jax.shard_map(
        per_device, mesh=mesh, in_specs=in_specs, out_specs=out_specs, check_vma=False
    )

    def run(*args):
        with jax.sharding.use_abstract_mesh(mesh.abstract_mesh):
            return mapped(*args)

    return run
```

```python
import functools

import jax
import jax.numpy as jnp
from jax import lax
from jax.experimental import pallas as pl
from jax.experimental.pallas import tpu as pltpu
from jax.sharding import PartitionSpec as P

AGE = 128
DT = 4
ITERS = 4
LANES = 128
WIN = DT + 3
MXU = 256
STEP = 8
SHARE = 4
ROWS = 2 * WIN * 16
CHUNKS = 4
LISTS = 4
VMEM_SPREAD = 40 * 1024 * 1024


f32 = jnp.float32
bf16 = jnp.bfloat16


def spline(frac):
    rest = 1.0 - frac
    cube = frac * frac * frac
    return (
        rest * rest * rest / 6.0,
        (3.0 * cube - 6.0 * frac * frac + 4.0) / 6.0,
        (-3.0 * cube + 3.0 * frac * frac + 3.0 * frac + 1.0) / 6.0,
        cube / 6.0,
    )


def spread_body(
    blocks,
    tiles,
    core_ref,
    tile_ref,
    age_hbm,
    off_hbm,
    code_hbm,
    age_frac_hbm,
    dur_frac_hbm,
    expo_hbm,
    claim_hbm,
    keep_ref,
    send_ref,
    age_ref,
    off_ref,
    code_ref,
    age_frac_ref,
    dur_frac_ref,
    expo_ref,
    claim_ref,
    base_s,
    group_s,
    code_s,
    weight_s,
    term_s,
    acc_s,
    order_s,
    steps_s,
    *places_and_sems,
):
    at, sems = places_and_sems[:LISTS], places_and_sems[LISTS]
    slab = 8
    dur = tiles * DT
    part = blocks // CHUNKS
    quarter = blocks // LISTS
    sources = (age_hbm, off_hbm, code_hbm, age_frac_hbm, dur_frac_hbm, expo_hbm, claim_hbm)
    targets = (age_ref, off_ref, code_ref, age_frac_ref, dur_frac_ref, expo_ref, claim_ref)
    copies = []
    for c in range(CHUNKS):
        rows = pl.ds(c * part, part)
        copies.append(
            [
                pltpu.make_async_copy(source.at[rows], target.at[rows], sems.at[c, k])
                for k, (source, target) in enumerate(zip(sources, targets))
            ]
        )
        for copy in copies[-1]:
            copy.start()

    def clear(t, _):
        for place in at:
            place[t] = 0
        return 0

    lax.fori_loop(0, tiles, clear, 0)

    def tally(i, _):
        for j in range(2):
            for k, place in enumerate(at):
                t = tile_ref[k * quarter + i * 2 + j]
                place[t] = place[t] + 1
        return 0

    lax.fori_loop(0, quarter // 2, tally, 0)

    def starts(t, start):
        end = start
        for place in at:
            count = place[t]
            place[t] = end
            end = end + count
        for j in range(STEP - 1):
            order_s[end + j] = blocks
        steps = lax.div(end - start + (STEP - 1), STEP)
        steps_s[t] = steps
        return start + steps * STEP

    padded = lax.fori_loop(0, tiles, starts, jnp.int32(0))
    for j in range(STEP):
        order_s[padded + j] = blocks

    acc_s[...] = jnp.zeros_like(acc_s)
    blank = jnp.zeros((slab, LANES), f32)
    pad = pl.ds(blocks, slab)
    base_s[pad] = blank
    group_s[pad] = blank
    code_s[pad] = blank - 1.0
    for place in range(4):
        weight_s[place, pad] = blank
    for row in range(2 * WIN):
        term_s[row, pad] = blank

    def prepare(i, _):
        rows = pl.ds(pl.multiple_of(i * slab, slab), slab)
        first = age_ref[rows] - 1
        base_s[rows] = (first & 15).astype(f32)
        group_s[rows] = (first >> 4).astype(f32)
        code_s[rows] = code_ref[rows].astype(f32)
        for place, weight in enumerate(spline(age_frac_ref[rows])):
            weight_s[place, rows] = weight.astype(bf16).astype(f32)
        dur_w = spline(dur_frac_ref[rows])
        offset = off_ref[rows]
        is_offset = [offset == o for o in range(DT)]
        for channel, value in enumerate((expo_ref[rows], claim_ref[rows])):
            terms = [(w * value).astype(bf16).astype(f32) for w in dur_w]
            for cell in range(WIN):
                term = jnp.zeros((slab, LANES), f32)
                for o in range(DT):
                    if 0 <= cell - o < 4:
                        term = jnp.where(is_offset[o], terms[cell - o], term)
                term_s[channel * WIN + cell, rows] = term
        for j in range(2):
            for k, place in enumerate(at):
                block = k * quarter + i * 2 + j
                t = tile_ref[block]
                spot = place[t]
                order_s[spot] = block
                place[t] = spot + 1
        return 0

    for c in range(CHUNKS):
        for copy in copies[c]:
            copy.wait()
        lax.fori_loop(c * (part // slab), (c + 1) * (part // slab), prepare, 0)

    row16 = lax.broadcasted_iota(jnp.int32, (16, LANES), 0)
    row16b = row16.astype(f32).astype(bf16)
    codes = [(half * 8 + (row16 & 7)).astype(f32).astype(bf16) for half in range(2)]
    zero = jnp.zeros((16, LANES), bf16)

    def spread_row(ref, r, count=16):
        return jnp.broadcast_to(ref[pl.ds(r, 1), :], (count, LANES))

    def build(r, left_ref):
        base = spread_row(base_s, r).astype(bf16)
        group = spread_row(group_s, r).astype(bf16)
        weights = [spread_row(weight_s.at[place], r).astype(bf16) for place in range(4)]
        ahead = row16b - base
        wraps = ahead < 0
        place = jnp.where(wraps, ahead + 16, ahead)
        pattern = zero
        for k in range(4):
            pattern = jnp.where(place == k, weights[k], pattern)
        owner = jnp.where(wraps, group + 1, group)
        code = spread_row(code_s, r).astype(bf16)
        masks = [code == c for c in codes]
        for cell in range(WIN):
            expo = spread_row(term_s.at[cell], r, 8)
            claim = spread_row(term_s.at[WIN + cell], r, 8)
            both = jnp.concatenate([expo, claim], axis=0).astype(bf16)
            for half in range(2):
                left_ref[half * WIN + cell] = jnp.where(masks[half], both, zero)
        return jnp.concatenate(
            [jnp.where(owner == a, pattern, zero) for a in range(AGE // 16)], axis=0
        )

    def all_tiles(left_a, left_b, *accs):
        def fill(first, left, stage):
            for unit in range(2):
                ages = [
                    build(order_s[first + 4 * unit + j], left.at[4 * unit + j]) for j in range(4)
                ]
                pairs = [jnp.concatenate(ages[j : j + 2], axis=1) for j in (0, 2)]
                pltpu.matmul_push_rhs(
                    jnp.concatenate(pairs, axis=0), stage, unit, transpose=True
                )

        def multiply(left, stage):
            for pair in range(2):
                for unit in range(2):
                    j = 4 * unit + 2 * pair
                    rows = [left[j + k].reshape(ROWS, LANES) for k in range(2)]
                    pltpu.matmul_acc_lhs(
                        accs[2 * unit + pair],
                        jnp.concatenate(rows, axis=1),
                        load_staged_rhs=stage if pair == 0 else None,
                    )

        def take():
            totals = [pltpu.matmul_pop(acc) for acc in accs]
            return (totals[0][:, :AGE] + totals[1][:, AGE:]) + (
                totals[2][:, :AGE] + totals[3][:, AGE:]
            )

        fill(0, left_a, 0)

        def one_tile(t, done):
            steps = steps_s[t]
            odd = steps & 1

            @pl.when(steps > 0)
            def _():
                @pl.when(odd == 1)
                def _():
                    multiply(left_a, 0)
                    fill((done + 1) * STEP, left_a, 0)

                def two_steps(s, _):
                    first = (done + odd + 2 * s) * STEP
                    fill(first + STEP, left_b, 1)
                    multiply(left_a, 0)
                    fill(first + 2 * STEP, left_a, 0)
                    multiply(left_b, 1)
                    return 0

                lax.fori_loop(0, steps >> 1, two_steps, 0)
                total = take().reshape(2, WIN, 2, 8, LANES)
                for half in range(2):
                    for cell in range(WIN):
                        for channel in range(2):
                            acc_s[half * 2 + channel, t * DT + cell] += total[half, cell, channel]

            return done + steps

        lax.fori_loop(0, tiles, one_tile, jnp.int32(0))
        multiply(left_a, 0)
        acc_s[0, 0] = take()[:8]

    pl.run_scoped(
        all_tiles,
        *[pltpu.VMEM((STEP, ROWS // 16, 16, LANES), bf16)] * 2,
        *[pltpu.ACC(unit)((ROWS, MXU), f32) for unit in (0, 0, 1, 1)],
    )

    low = lax.broadcasted_iota(jnp.int32, (8, LANES), 0) < 4
    mine = core_ref[0]
    for whose, half in enumerate((mine, 1 - mine)):
        expo = acc_s[half * 2, 1 : dur + 1]
        claim = acc_s[half * 2 + 1, 1 : dur + 1]
        quarters = (
            jnp.where(low, expo, pltpu.roll(claim, 4, 1)),
            jnp.where(low, pltpu.roll(expo, 4, 1), claim),
        )
        for q in range(2):
            if whose == 0:
                keep_ref[q] = quarters[q]
            else:
                send_ref[pl.ds(q * dur, dur)] = quarters[q]
    for channel in range(2):
        pooled = jnp.sum(
            acc_s[channel, 1 : dur + 1] + acc_s[2 + channel, 1 : dur + 1], axis=1
        )
        base = 2 * dur + channel * (dur // 8)
        send_ref[pl.ds(base, dur // 8)] = pooled.reshape(dur // 8, 8, LANES)


def spread(core, tile_ids, fields, tiles):
    blocks = tile_ids.shape[0]
    assert blocks % (8 * CHUNKS) == 0
    dur = tiles * DT
    rows = blocks + 8
    vmem = pl.BlockSpec(memory_space=pltpu.VMEM)
    smem = pl.BlockSpec(memory_space=pltpu.SMEM)
    hbm = pl.BlockSpec(memory_space=pltpu.HBM)
    return pl.pallas_call(
        functools.partial(spread_body, blocks, tiles),
        out_shape=(
            jax.ShapeDtypeStruct((2, dur, 8, LANES), f32),
            jax.ShapeDtypeStruct((2 * dur + 2 * (dur // 8), 8, LANES), f32),
        ),
        in_specs=[smem, smem] + [hbm] * 7,
        out_specs=(vmem, vmem),
        scratch_shapes=[
            *[pltpu.VMEM((blocks, LANES), jnp.int32)] * 3,
            *[pltpu.VMEM((blocks, LANES), f32)] * 4,
            pltpu.VMEM((rows, LANES), f32),
            pltpu.VMEM((rows, LANES), f32),
            pltpu.VMEM((rows, LANES), f32),
            pltpu.VMEM((4, rows, LANES), f32),
            pltpu.VMEM((2 * WIN, rows, LANES), f32),
            pltpu.VMEM((4, dur + 3, 8, LANES), f32),
            pltpu.SMEM((blocks + STEP * tiles + 2 * STEP,), jnp.int32),
            *[pltpu.SMEM((tiles,), jnp.int32)] * (LISTS + 1),
            pltpu.SemaphoreType.DMA((CHUNKS, 7)),
        ],
        compiler_params=pltpu.CompilerParams(vmem_limit_bytes=VMEM_SPREAD),
        name="spread",
    )(core, tile_ids, *fields)


def smooth_body(
    dur,
    where_ref,
    age_w_ref,
    dur_w_ref,
    cred_ref,
    grid_a_ref,
    grid_b_ref,
    pool_a_ref,
    pool_b_ref,
    out_ref,
    prior_s,
    x_s,
    r_s,
):
    half = dur // 2
    slot, high = where_ref[0], where_ref[1]
    sub = lax.broadcasted_iota(jnp.int32, (8, LANES), 0)
    lane = lax.broadcasted_iota(jnp.int32, (1, 8, LANES), 2)
    low = sub < 4

    def swap(v):
        return pltpu.roll(v, 4, v.ndim - 2)

    def per_transition(ref):
        value = jnp.full((8, LANES), ref[slot], f32)
        for t in range(1, 4):
            value = jnp.where((sub & 3) == t, ref[slot + t], value)
        return value

    weight_a, weight_d, cred = map(per_transition, (age_w_ref, dur_w_ref, cred_ref))
    pool = pool_a_ref[...] + pool_b_ref[...]
    eighth = dur // 8
    prior_s[...] = (pool[eighth:] / (1.0 + pool[:eighth])).reshape(dur, LANES)
    grid = grid_a_ref[...] + grid_b_ref[...]
    top, bottom = grid[:half], grid[half:]
    diagonal = jnp.where(low, top, swap(bottom)) + cred
    claims = jnp.where(low, swap(top), bottom)
    prior = jnp.stack(
        [
            jnp.where(
                low,
                jnp.broadcast_to(prior_s[pl.ds(d, 1), :], (8, LANES)),
                jnp.broadcast_to(prior_s[pl.ds(half + d, 1), :], (8, LANES)),
            )
            for d in range(half)
        ]
    )
    rhs = claims + cred * prior

    def operate(v):
        y = v - 2.0 * pltpu.roll(v, LANES - 1, 2) + pltpu.roll(v, LANES - 2, 2)
        y = jnp.where(lane < AGE - 2, y, 0.0)
        along_age = y - 2.0 * pltpu.roll(y, 1, 2) + pltpu.roll(y, 2, 2)
        longer = jnp.concatenate([v, swap(v[:2])], axis=0)
        y = longer[:half] - 2.0 * longer[1 : half + 1] + longer[2 : half + 2]
        y = jnp.concatenate([y[: half - 2], jnp.where(low, y[half - 2 :], 0.0)], axis=0)
        longer = jnp.concatenate([jnp.where(low, 0.0, swap(y[half - 2 :])), y], axis=0)
        along_dur = longer[2:] - 2.0 * longer[1 : half + 1] + longer[:half]
        return diagonal * v + weight_a * along_age + weight_d * along_dur

    def inner(a, b):
        part = jnp.sum(a * b, axis=0)
        part = part + swap(part)
        return jnp.sum(part, axis=1, keepdims=True)

    x = jnp.zeros_like(rhs)
    r = rhs
    p = rhs
    norm = inner(r, r)
    for turn in range(ITERS):
        image = operate(p)
        alpha = norm / inner(p, image)
        x = x + alpha * p
        r = r - alpha * image
        if turn < ITERS - 1:
            after = inner(r, r)
            p = r + (after / norm) * p
            norm = after
    x_s[...] = x
    r_s[...] = r
    span = SHARE * DT
    in_low = high * span < half
    start = jnp.where(in_low, high * span, high * span - half)
    for dest in range(SHARE):
        for d in range(DT):
            xv = x_s[start + dest * DT + d]
            rv = r_s[start + dest * DT + d]
            row = jnp.where(
                in_low, jnp.where(low, xv, swap(rv)), jnp.where(low, swap(xv), rv)
            )
            out_ref[dest, pl.ds(d, 8, stride=DT), :] = row


def smooth(where, weights, grid_a, grid_b, pool_a, pool_b):
    dur = grid_a.shape[0]
    vmem = pl.BlockSpec(memory_space=pltpu.VMEM)
    smem = pl.BlockSpec(memory_space=pltpu.SMEM)
    return pl.pallas_call(
        functools.partial(smooth_body, dur),
        out_shape=jax.ShapeDtypeStruct((SHARE, 8 * DT, LANES), f32),
        in_specs=[smem] * 4 + [vmem] * 4,
        out_specs=vmem,
        scratch_shapes=[
            pltpu.VMEM((dur, LANES), f32),
            pltpu.VMEM((dur // 2, 8, LANES), f32),
            pltpu.VMEM((dur // 2, 8, LANES), f32),
        ],
        compiler_params=pltpu.CompilerParams(vmem_limit_bytes=32 * 1024 * 1024),
        name="smooth",
    )(where, *weights, grid_a, grid_b, pool_a, pool_b)


def gather_body(me_ref, own_ref, one_ref, two_ref, three_ref, x_ref, r_ref):
    me = me_ref[0]
    for k, ref in enumerate((own_ref, one_ref, two_ref, three_ref)):
        other = me ^ k
        slot = (other & 1) * 2 + (other >> 1)
        got = ref[me] if k == 0 else ref[...]
        x_ref[slot] = got[: 4 * DT]
        r_ref[slot] = got[4 * DT :]


def gather(me, own, others):
    vmem = pl.BlockSpec(memory_space=pltpu.VMEM)
    smem = pl.BlockSpec(memory_space=pltpu.SMEM)
    shape = jax.ShapeDtypeStruct((SHARE, 4 * DT, LANES), f32)
    return pl.pallas_call(
        gather_body,
        out_shape=(shape, shape),
        in_specs=[smem] + [vmem] * 4,
        out_specs=(vmem, vmem),
        compiler_params=pltpu.CompilerParams(vmem_limit_bytes=4 * 1024 * 1024),
        name="gather",
    )(me, own, *others)


def swap_with(value, axis, bit):
    size = lax.axis_size(axis)
    return lax.ppermute(value, axis, [(i, i ^ bit) for i in range(size)])


def bits_of(size):
    bits = [1 << k for k in range(size.bit_length() - 1)]
    assert 1 << len(bits) == size, size
    return bits


def per_device(
    age_cell,
    dur_cell,
    trans_code,
    age_frac,
    dur_frac,
    exposure,
    claims,
    block_tile,
    smooth_age,
    smooth_dur,
    credibility,
):
    trans_dev = smooth_age.shape[0]
    tiles = lax.axis_size("tile")
    groups = lax.axis_size("tg")
    dur = tiles * DT
    assert trans_dev == 4 * SHARE and tiles % 8 == 0
    here = lax.axis_index("tile")
    core, near, high = here & 1, (here >> 1) & 1, here >> 2
    tile_ids = pltpu.with_memory_space_constraint(block_tile.reshape(-1), pltpu.HBM)
    blocks = tile_ids.shape[0]
    fields = [
        pltpu.with_memory_space_constraint(field.reshape(blocks, LANES), pltpu.HBM)
        for field in (age_cell, dur_cell, trans_code, age_frac, dur_frac, exposure, claims)
    ]
    keep, send = spread(core.reshape(1), tile_ids, fields, tiles)
    got = swap_with(send, "tile", 1)
    pool = send[2 * dur :] + got[2 * dur :]
    got = got[: 2 * dur].reshape(keep.shape)

    def quarter(at):
        return lax.dynamic_index_in_dim(keep, at, 0, False) + lax.dynamic_index_in_dim(
            got, at, 0, False
        )

    grid = quarter(near) + swap_with(quarter(1 - near), "tile", 2)
    tile_bits = bits_of(tiles)
    pool_bits = [("tg", bit) for bit in bits_of(groups)] + [("tile", bit) for bit in tile_bits[1:]]
    for axis, bit in pool_bits[:-1]:
        pool = pool + swap_with(pool, axis, bit)
    pool_other = swap_with(pool, *pool_bits[-1])
    for bit in tile_bits[2:-1]:
        grid = grid + swap_with(grid, "tile", bit)
    grid_other = swap_with(grid, "tile", tile_bits[-1])
    slot = core * 8 + near * 4
    own = smooth(
        jnp.stack([slot, high]),
        (smooth_age, smooth_dur, credibility),
        grid,
        grid_other,
        pool,
        pool_other,
    )
    me = here & 3
    others = [
        swap_with(lax.dynamic_index_in_dim(own, me ^ k, 0, False), "tile", k) for k in (1, 2, 3)
    ]
    smoothed, residual = gather(me.reshape(1), own, others)
    shape = (trans_dev, DT, AGE)
    return smoothed.reshape(shape), residual.reshape(shape)


def solution(mesh):
    records = P("tg", "tile")
    in_specs = (records,) * 7 + (P("tg", "tile", None),) + (P("tg"),) * 3
    out_specs = (P("tg", "tile", None), P("tg", "tile", None))
    mapped = jax.shard_map(
        per_device, mesh=mesh, in_specs=in_specs, out_specs=out_specs, check_vma=False
    )

    def run(*args):
        with jax.sharding.use_abstract_mesh(mesh.abstract_mesh):
            return mapped(*args)

    return run
```

```python
import functools

import jax
import jax.numpy as jnp
from jax import lax
from jax.experimental import pallas as pl
from jax.experimental.pallas import tpu as pltpu
from jax.sharding import PartitionSpec as P

AGE = 128
DT = 4
ITERS = 4
LANES = 128
WIN = DT + 3
MXU = 256
STEP = 8
SHARE = 4
ROWS = 2 * WIN * 16
CHUNKS = 2
LISTS = 4
SLAB = 16
TALLY = 8
VMEM_SPREAD = 40 * 1024 * 1024


f32 = jnp.float32
bf16 = jnp.bfloat16


def spline(frac):
    rest = 1.0 - frac
    cube = frac * frac * frac
    return (
        rest * rest * rest / 6.0,
        (3.0 * cube - 6.0 * frac * frac + 4.0) / 6.0,
        (-3.0 * cube + 3.0 * frac * frac + 3.0 * frac + 1.0) / 6.0,
        cube / 6.0,
    )


def spread_body(
    blocks,
    tiles,
    core_ref,
    tile_ref,
    age_hbm,
    off_hbm,
    code_hbm,
    age_frac_hbm,
    dur_frac_hbm,
    expo_hbm,
    claim_hbm,
    keep_ref,
    send_ref,
    age_ref,
    off_ref,
    code_ref,
    age_frac_ref,
    dur_frac_ref,
    expo_ref,
    claim_ref,
    base_s,
    group_s,
    code_s,
    weight_s,
    term_s,
    acc_s,
    order_s,
    steps_s,
    *places_and_sems,
):
    at, sems = places_and_sems[:LISTS], places_and_sems[LISTS]
    dur = tiles * DT
    part = blocks // CHUNKS
    quarter = blocks // LISTS
    sources = (age_hbm, off_hbm, code_hbm, age_frac_hbm, dur_frac_hbm, expo_hbm, claim_hbm)
    targets = (age_ref, off_ref, code_ref, age_frac_ref, dur_frac_ref, expo_ref, claim_ref)
    copies = []
    for c in range(CHUNKS):
        rows = pl.ds(c * part, part)
        copies.append(
            [
                pltpu.make_async_copy(source.at[rows], target.at[rows], sems.at[c, k])
                for k, (source, target) in enumerate(zip(sources, targets))
            ]
        )
        for copy in copies[-1]:
            copy.start()

    def clear(t, _):
        for place in at:
            place[t] = 0
        return 0

    lax.fori_loop(0, tiles, clear, 0)

    def tally(i, _):
        for j in range(TALLY):
            for k, place in enumerate(at):
                t = tile_ref[k * quarter + i * TALLY + j]
                place[t] = place[t] + 1
        return 0

    lax.fori_loop(0, quarter // TALLY, tally, 0)

    def starts(t, start):
        end = start
        for place in at:
            count = place[t]
            place[t] = end
            end = end + count
        for j in range(STEP - 1):
            order_s[end + j] = blocks
        steps = lax.div(end - start + (STEP - 1), STEP)
        steps_s[t] = steps
        return start + steps * STEP

    padded = lax.fori_loop(0, tiles, starts, jnp.int32(0))
    for j in range(STEP):
        order_s[padded + j] = blocks

    acc_s[...] = jnp.zeros_like(acc_s)
    blank = jnp.zeros((8, LANES), f32)
    pad = pl.ds(blocks, 8)
    base_s[pad] = blank
    group_s[pad] = blank
    code_s[pad] = blank - 1.0
    for place in range(4):
        weight_s[place, pad] = blank
    for row in range(2 * WIN):
        term_s[row, pad] = blank

    def prepare(i, _):
        rows = pl.ds(pl.multiple_of(i * SLAB, SLAB), SLAB)
        first = age_ref[rows] - 1
        base_s[rows] = (first & 15).astype(f32)
        group_s[rows] = (first >> 4).astype(f32)
        code_s[rows] = code_ref[rows].astype(f32)
        for place, weight in enumerate(spline(age_frac_ref[rows])):
            weight_s[place, rows] = weight.astype(bf16).astype(f32)
        dur_w = spline(dur_frac_ref[rows])
        offset = off_ref[rows]
        is_offset = [offset == o for o in range(DT)]
        for channel, value in enumerate((expo_ref[rows], claim_ref[rows])):
            terms = [(w * value).astype(bf16).astype(f32) for w in dur_w]
            for cell in range(WIN):
                term = jnp.zeros((SLAB, LANES), f32)
                for o in range(DT):
                    if 0 <= cell - o < 4:
                        term = jnp.where(is_offset[o], terms[cell - o], term)
                term_s[channel * WIN + cell, rows] = term
        for j in range(SLAB // LISTS):
            for k, place in enumerate(at):
                block = k * quarter + i * (SLAB // LISTS) + j
                t = tile_ref[block]
                spot = place[t]
                order_s[spot] = block
                place[t] = spot + 1
        return 0

    for c in range(CHUNKS):
        for copy in copies[c]:
            copy.wait()
        lax.fori_loop(c * (part // SLAB), (c + 1) * (part // SLAB), prepare, 0)

    row16 = lax.broadcasted_iota(jnp.int32, (16, LANES), 0)
    row16b = row16.astype(f32).astype(bf16)
    codes = [(half * 8 + (row16 & 7)).astype(f32).astype(bf16) for half in range(2)]
    zero = jnp.zeros((16, LANES), bf16)

    def spread_row(ref, r, count=16):
        return jnp.broadcast_to(ref[pl.ds(r, 1), :], (count, LANES))

    def build(r, left_ref):
        base = spread_row(base_s, r).astype(bf16)
        group = spread_row(group_s, r).astype(bf16)
        weights = [spread_row(weight_s.at[place], r).astype(bf16) for place in range(4)]
        ahead = row16b - base
        wraps = ahead < 0
        place = jnp.where(wraps, ahead + 16, ahead)
        pattern = zero
        for k in range(4):
            pattern = jnp.where(place == k, weights[k], pattern)
        owner = jnp.where(wraps, group + 1, group)
        code = spread_row(code_s, r).astype(bf16)
        masks = [code == c for c in codes]
        for cell in range(WIN):
            expo = spread_row(term_s.at[cell], r, 8)
            claim = spread_row(term_s.at[WIN + cell], r, 8)
            both = jnp.concatenate([expo, claim], axis=0).astype(bf16)
            for half in range(2):
                left_ref[half * WIN + cell] = jnp.where(masks[half], both, zero)
        return jnp.concatenate(
            [jnp.where(owner == a, pattern, zero) for a in range(AGE // 16)], axis=0
        )

    def all_tiles(left_a, left_b, *accs):
        def fill(first, left, stage):
            for unit in range(2):
                ages = [
                    build(order_s[first + 4 * unit + j], left.at[4 * unit + j]) for j in range(4)
                ]
                pairs = [jnp.concatenate(ages[j : j + 2], axis=1) for j in (0, 2)]
                pltpu.matmul_push_rhs(
                    jnp.concatenate(pairs, axis=0), stage, unit, transpose=True
                )

        def multiply(left, stage):
            for pair in range(2):
                for unit in range(2):
                    j = 4 * unit + 2 * pair
                    rows = [left[j + k].reshape(ROWS, LANES) for k in range(2)]
                    pltpu.matmul_acc_lhs(
                        accs[2 * unit + pair],
                        jnp.concatenate(rows, axis=1),
                        load_staged_rhs=stage if pair == 0 else None,
                    )

        def take():
            totals = [pltpu.matmul_pop(acc) for acc in accs]
            return (totals[0][:, :AGE] + totals[1][:, AGE:]) + (
                totals[2][:, :AGE] + totals[3][:, AGE:]
            )

        fill(0, left_a, 0)

        def one_tile(t, done):
            steps = steps_s[t]
            odd = steps & 1

            @pl.when(steps > 0)
            def _():
                @pl.when(odd == 1)
                def _():
                    multiply(left_a, 0)
                    fill((done + 1) * STEP, left_a, 0)

                def two_steps(s, _):
                    first = (done + odd + 2 * s) * STEP
                    multiply(left_a, 0)
                    fill(first + STEP, left_b, 1)
                    multiply(left_b, 1)
                    fill(first + 2 * STEP, left_a, 0)
                    return 0

                lax.fori_loop(0, steps >> 1, two_steps, 0)
                total = take().reshape(2, WIN, 2, 8, LANES)
                for half in range(2):
                    for cell in range(WIN):
                        for channel in range(2):
                            acc_s[half * 2 + channel, t * DT + cell] += total[half, cell, channel]

            return done + steps

        lax.fori_loop(0, tiles, one_tile, jnp.int32(0))
        multiply(left_a, 0)
        acc_s[0, 0] = take()[:8]

    pl.run_scoped(
        all_tiles,
        *[pltpu.VMEM((STEP, ROWS // 16, 16, LANES), bf16)] * 2,
        *[pltpu.ACC(unit)((ROWS, MXU), f32) for unit in (0, 0, 1, 1)],
    )

    low = lax.broadcasted_iota(jnp.int32, (8, LANES), 0) < 4
    mine = core_ref[0]
    for whose, half in enumerate((mine, 1 - mine)):
        expo = acc_s[half * 2, 1 : dur + 1]
        claim = acc_s[half * 2 + 1, 1 : dur + 1]
        quarters = (
            jnp.where(low, expo, pltpu.roll(claim, 4, 1)),
            jnp.where(low, pltpu.roll(expo, 4, 1), claim),
        )
        for q in range(2):
            if whose == 0:
                keep_ref[q] = quarters[q]
            else:
                send_ref[pl.ds(q * dur, dur)] = quarters[q]
    for channel in range(2):
        pooled = jnp.sum(
            acc_s[channel, 1 : dur + 1] + acc_s[2 + channel, 1 : dur + 1], axis=1
        )
        base = 2 * dur + channel * (dur // 8)
        send_ref[pl.ds(base, dur // 8)] = pooled.reshape(dur // 8, 8, LANES)


def spread(core, tile_ids, fields, tiles):
    blocks = tile_ids.shape[0]
    assert blocks % (SLAB * CHUNKS) == 0 and blocks % (LISTS * TALLY) == 0
    dur = tiles * DT
    rows = blocks + 8
    vmem = pl.BlockSpec(memory_space=pltpu.VMEM)
    smem = pl.BlockSpec(memory_space=pltpu.SMEM)
    hbm = pl.BlockSpec(memory_space=pltpu.HBM)
    return pl.pallas_call(
        functools.partial(spread_body, blocks, tiles),
        out_shape=(
            jax.ShapeDtypeStruct((2, dur, 8, LANES), f32),
            jax.ShapeDtypeStruct((2 * dur + 2 * (dur // 8), 8, LANES), f32),
        ),
        in_specs=[smem, smem] + [hbm] * 7,
        out_specs=(vmem, vmem),
        scratch_shapes=[
            *[pltpu.VMEM((blocks, LANES), jnp.int32)] * 3,
            *[pltpu.VMEM((blocks, LANES), f32)] * 4,
            pltpu.VMEM((rows, LANES), f32),
            pltpu.VMEM((rows, LANES), f32),
            pltpu.VMEM((rows, LANES), f32),
            pltpu.VMEM((4, rows, LANES), f32),
            pltpu.VMEM((2 * WIN, rows, LANES), f32),
            pltpu.VMEM((4, dur + 3, 8, LANES), f32),
            pltpu.SMEM((blocks + STEP * tiles + 2 * STEP,), jnp.int32),
            *[pltpu.SMEM((tiles,), jnp.int32)] * (LISTS + 1),
            pltpu.SemaphoreType.DMA((CHUNKS, 7)),
        ],
        compiler_params=pltpu.CompilerParams(vmem_limit_bytes=VMEM_SPREAD),
        name="spread",
    )(core, tile_ids, *fields)


def smooth_body(
    dur,
    where_ref,
    age_w_ref,
    dur_w_ref,
    cred_ref,
    grid_a_ref,
    grid_b_ref,
    pool_a_ref,
    pool_b_ref,
    out_ref,
    prior_s,
    x_s,
    r_s,
):
    half = dur // 2
    slot, high = where_ref[0], where_ref[1]
    sub = lax.broadcasted_iota(jnp.int32, (8, LANES), 0)
    lane = lax.broadcasted_iota(jnp.int32, (1, 8, LANES), 2)
    low = sub < 4

    def swap(v):
        return pltpu.roll(v, 4, v.ndim - 2)

    def per_transition(ref):
        value = jnp.full((8, LANES), ref[slot], f32)
        for t in range(1, 4):
            value = jnp.where((sub & 3) == t, ref[slot + t], value)
        return value

    weight_a, weight_d, cred = map(per_transition, (age_w_ref, dur_w_ref, cred_ref))
    pool = pool_a_ref[...] + pool_b_ref[...]
    eighth = dur // 8
    prior_s[...] = (pool[eighth:] / (1.0 + pool[:eighth])).reshape(dur, LANES)
    grid = grid_a_ref[...] + grid_b_ref[...]
    top, bottom = grid[:half], grid[half:]
    diagonal = jnp.where(low, top, swap(bottom)) + cred
    claims = jnp.where(low, swap(top), bottom)
    prior = jnp.stack(
        [
            jnp.where(
                low,
                jnp.broadcast_to(prior_s[pl.ds(d, 1), :], (8, LANES)),
                jnp.broadcast_to(prior_s[pl.ds(half + d, 1), :], (8, LANES)),
            )
            for d in range(half)
        ]
    )
    rhs = claims + cred * prior

    def operate(v):
        y = v - 2.0 * pltpu.roll(v, LANES - 1, 2) + pltpu.roll(v, LANES - 2, 2)
        y = jnp.where(lane < AGE - 2, y, 0.0)
        along_age = y - 2.0 * pltpu.roll(y, 1, 2) + pltpu.roll(y, 2, 2)
        longer = jnp.concatenate([v, swap(v[:2])], axis=0)
        y = longer[:half] - 2.0 * longer[1 : half + 1] + longer[2 : half + 2]
        y = jnp.concatenate([y[: half - 2], jnp.where(low, y[half - 2 :], 0.0)], axis=0)
        longer = jnp.concatenate([jnp.where(low, 0.0, swap(y[half - 2 :])), y], axis=0)
        along_dur = longer[2:] - 2.0 * longer[1 : half + 1] + longer[:half]
        return diagonal * v + weight_a * along_age + weight_d * along_dur

    def inner(a, b):
        part = jnp.sum(a * b, axis=0)
        part = part + swap(part)
        return jnp.sum(part, axis=1, keepdims=True)

    x = jnp.zeros_like(rhs)
    r = rhs
    p = rhs
    norm = inner(r, r)
    for turn in range(ITERS):
        image = operate(p)
        alpha = norm / inner(p, image)
        x = x + alpha * p
        r = r - alpha * image
        if turn < ITERS - 1:
            after = inner(r, r)
            p = r + (after / norm) * p
            norm = after
    x_s[...] = x
    r_s[...] = r
    span = SHARE * DT
    in_low = high * span < half
    start = jnp.where(in_low, high * span, high * span - half)
    for dest in range(SHARE):
        for d in range(DT):
            xv = x_s[start + dest * DT + d]
            rv = r_s[start + dest * DT + d]
            row = jnp.where(
                in_low, jnp.where(low, xv, swap(rv)), jnp.where(low, swap(xv), rv)
            )
            out_ref[dest, pl.ds(d, 8, stride=DT), :] = row


def smooth(where, weights, grid_a, grid_b, pool_a, pool_b):
    dur = grid_a.shape[0]
    vmem = pl.BlockSpec(memory_space=pltpu.VMEM)
    smem = pl.BlockSpec(memory_space=pltpu.SMEM)
    return pl.pallas_call(
        functools.partial(smooth_body, dur),
        out_shape=jax.ShapeDtypeStruct((SHARE, 8 * DT, LANES), f32),
        in_specs=[smem] * 4 + [vmem] * 4,
        out_specs=vmem,
        scratch_shapes=[
            pltpu.VMEM((dur, LANES), f32),
            pltpu.VMEM((dur // 2, 8, LANES), f32),
            pltpu.VMEM((dur // 2, 8, LANES), f32),
        ],
        compiler_params=pltpu.CompilerParams(vmem_limit_bytes=32 * 1024 * 1024),
        name="smooth",
    )(where, *weights, grid_a, grid_b, pool_a, pool_b)


def gather_body(me_ref, own_ref, one_ref, two_ref, three_ref, x_ref, r_ref):
    me = me_ref[0]
    for k, ref in enumerate((own_ref, one_ref, two_ref, three_ref)):
        other = me ^ k
        slot = (other & 1) * 2 + (other >> 1)
        got = ref[me] if k == 0 else ref[...]
        x_ref[slot] = got[: 4 * DT]
        r_ref[slot] = got[4 * DT :]


def gather(me, own, others):
    vmem = pl.BlockSpec(memory_space=pltpu.VMEM)
    smem = pl.BlockSpec(memory_space=pltpu.SMEM)
    shape = jax.ShapeDtypeStruct((SHARE, 4 * DT, LANES), f32)
    return pl.pallas_call(
        gather_body,
        out_shape=(shape, shape),
        in_specs=[smem] + [vmem] * 4,
        out_specs=(vmem, vmem),
        compiler_params=pltpu.CompilerParams(vmem_limit_bytes=4 * 1024 * 1024),
        name="gather",
    )(me, own, *others)


def swap_with(value, axis, bit):
    size = lax.axis_size(axis)
    return lax.ppermute(value, axis, [(i, i ^ bit) for i in range(size)])


def bits_of(size):
    bits = [1 << k for k in range(size.bit_length() - 1)]
    assert 1 << len(bits) == size, size
    return bits


def per_device(
    age_cell,
    dur_cell,
    trans_code,
    age_frac,
    dur_frac,
    exposure,
    claims,
    block_tile,
    smooth_age,
    smooth_dur,
    credibility,
):
    trans_dev = smooth_age.shape[0]
    tiles = lax.axis_size("tile")
    groups = lax.axis_size("tg")
    dur = tiles * DT
    assert trans_dev == 4 * SHARE and tiles % 8 == 0
    here = lax.axis_index("tile")
    core, near, high = here & 1, (here >> 1) & 1, here >> 2
    tile_ids = pltpu.with_memory_space_constraint(block_tile.reshape(-1), pltpu.HBM)
    blocks = tile_ids.shape[0]
    fields = [
        pltpu.with_memory_space_constraint(field.reshape(blocks, LANES), pltpu.HBM)
        for field in (age_cell, dur_cell, trans_code, age_frac, dur_frac, exposure, claims)
    ]
    keep, send = spread(core.reshape(1), tile_ids, fields, tiles)
    got = swap_with(send, "tile", 1)
    pool = send[2 * dur :] + got[2 * dur :]
    got = got[: 2 * dur].reshape(keep.shape)

    def quarter(at):
        return lax.dynamic_index_in_dim(keep, at, 0, False) + lax.dynamic_index_in_dim(
            got, at, 0, False
        )

    grid = quarter(near) + swap_with(quarter(1 - near), "tile", 2)
    tile_bits = bits_of(tiles)
    pool_bits = [("tg", bit) for bit in bits_of(groups)] + [("tile", bit) for bit in tile_bits[1:]]
    for axis, bit in pool_bits[:-1]:
        pool = pool + swap_with(pool, axis, bit)
    pool_other = swap_with(pool, *pool_bits[-1])
    for bit in tile_bits[2:-1]:
        grid = grid + swap_with(grid, "tile", bit)
    grid_other = swap_with(grid, "tile", tile_bits[-1])
    slot = core * 8 + near * 4
    own = smooth(
        jnp.stack([slot, high]),
        (smooth_age, smooth_dur, credibility),
        grid,
        grid_other,
        pool,
        pool_other,
    )
    me = here & 3
    others = [
        swap_with(lax.dynamic_index_in_dim(own, me ^ k, 0, False), "tile", k) for k in (1, 2, 3)
    ]
    smoothed, residual = gather(me.reshape(1), own, others)
    shape = (trans_dev, DT, AGE)
    return smoothed.reshape(shape), residual.reshape(shape)


def solution(mesh):
    records = P("tg", "tile")
    in_specs = (records,) * 7 + (P("tg", "tile", None),) + (P("tg"),) * 3
    out_specs = (P("tg", "tile", None), P("tg", "tile", None))
    mapped = jax.shard_map(
        per_device, mesh=mesh, in_specs=in_specs, out_specs=out_specs, check_vma=False
    )

    def run(*args):
        with jax.sharding.use_abstract_mesh(mesh.abstract_mesh):
            return mapped(*args)

    return run
```

```python
import functools

import jax
import jax.numpy as jnp
from jax import lax
from jax.experimental import pallas as pl
from jax.experimental.pallas import tpu as pltpu
from jax.sharding import PartitionSpec as P


AGE = 128
DT = 4
ITERS = 4
LANES = 128
WIN = DT + 3
MXU = 256
STEP = 8
SHARE = 4
ROWS = 2 * WIN * 16
CHUNKS = 2
LISTS = 4
SLAB = 16
TALLY = 8
VMEM_SPREAD = 40 * 1024 * 1024


f32 = jnp.float32
bf16 = jnp.bfloat16


def spline(frac):
    rest = 1.0 - frac
    cube = frac * frac * frac
    return (
        rest * rest * rest / 6.0,
        (3.0 * cube - 6.0 * frac * frac + 4.0) / 6.0,
        (-3.0 * cube + 3.0 * frac * frac + 3.0 * frac + 1.0) / 6.0,
        cube / 6.0,
    )


def spread_body(
    blocks,
    tiles,
    tile_ref,
    age_hbm,
    off_hbm,
    code_hbm,
    age_frac_hbm,
    dur_frac_hbm,
    expo_hbm,
    claim_hbm,
    age_w_hbm,
    dur_w_hbm,
    cred_hbm,
    keep_ref,
    send_ref,
    weights_ref,
    age_ref,
    off_ref,
    code_ref,
    age_frac_ref,
    dur_frac_ref,
    expo_ref,
    claim_ref,
    base_s,
    group_s,
    code_s,
    weight_s,
    term_s,
    acc_s,
    order_s,
    steps_s,
    *places_and_sems,
):
    at, sems = places_and_sems[:LISTS], places_and_sems[LISTS]
    dur = tiles * DT
    part = blocks // CHUNKS
    quarter = blocks // LISTS
    sources = (age_hbm, off_hbm, code_hbm, age_frac_hbm, dur_frac_hbm, expo_hbm, claim_hbm)
    targets = (age_ref, off_ref, code_ref, age_frac_ref, dur_frac_ref, expo_ref, claim_ref)
    copies = []
    for c in range(CHUNKS):
        rows = pl.ds(c * part, part)
        copies.append(
            [
                pltpu.make_async_copy(source.at[rows], target.at[rows], sems.at[c, k])
                for k, (source, target) in enumerate(zip(sources, targets))
            ]
        )
        for copy in copies[-1]:
            copy.start()

    passed = [
        pltpu.make_async_copy(source, weights_ref.at[k], sems.at[CHUNKS, k])
        for k, source in enumerate((age_w_hbm, dur_w_hbm, cred_hbm))
    ]
    for copy in passed:
        copy.start()

    def clear(t, _):
        for place in at:
            place[t] = 0
        return 0

    lax.fori_loop(0, tiles, clear, 0)

    def tally(i, _):
        for j in range(TALLY):
            for k, place in enumerate(at):
                t = tile_ref[k * quarter + i * TALLY + j]
                place[t] = place[t] + 1
        return 0

    lax.fori_loop(0, quarter // TALLY, tally, 0)

    def starts(t, start):
        end = start
        for place in at:
            count = place[t]
            place[t] = end
            end = end + count
        for j in range(STEP - 1):
            order_s[end + j] = blocks
        steps = lax.div(end - start + (STEP - 1), STEP)
        steps_s[t] = steps
        return start + steps * STEP

    padded = lax.fori_loop(0, tiles, starts, jnp.int32(0))
    for j in range(STEP):
        order_s[padded + j] = blocks

    acc_s[...] = jnp.zeros_like(acc_s)
    blank = jnp.zeros((8, LANES), f32)
    pad = pl.ds(blocks, 8)
    base_s[pad] = blank
    group_s[pad] = blank
    code_s[pad] = blank - 1.0
    for place in range(4):
        weight_s[place, pad] = blank
    for row in range(2 * WIN):
        term_s[row, pad] = blank

    def prepare(i, _):
        rows = pl.ds(pl.multiple_of(i * SLAB, SLAB), SLAB)
        first = age_ref[rows] - 1
        base_s[rows] = (first & 15).astype(f32)
        group_s[rows] = (first >> 4).astype(f32)
        code_s[rows] = code_ref[rows].astype(f32)
        for place, weight in enumerate(spline(age_frac_ref[rows])):
            weight_s[place, rows] = weight.astype(bf16).astype(f32)
        dur_w = spline(dur_frac_ref[rows])
        offset = off_ref[rows]
        is_offset = [offset == o for o in range(DT)]
        for channel, value in enumerate((expo_ref[rows], claim_ref[rows])):
            terms = [(w * value).astype(bf16).astype(f32) for w in dur_w]
            for cell in range(WIN):
                term = jnp.zeros((SLAB, LANES), f32)
                for o in range(DT):
                    if 0 <= cell - o < 4:
                        term = jnp.where(is_offset[o], terms[cell - o], term)
                term_s[channel * WIN + cell, rows] = term
        for j in range(SLAB // LISTS):
            for k, place in enumerate(at):
                block = k * quarter + i * (SLAB // LISTS) + j
                t = tile_ref[block]
                spot = place[t]
                order_s[spot] = block
                place[t] = spot + 1
        return 0

    for c in range(CHUNKS):
        for copy in copies[c]:
            copy.wait()
        lax.fori_loop(c * (part // SLAB), (c + 1) * (part // SLAB), prepare, 0)

    row16 = lax.broadcasted_iota(jnp.int32, (16, LANES), 0)
    row16b = row16.astype(f32).astype(bf16)
    codes = [(half * 8 + (row16 & 7)).astype(f32).astype(bf16) for half in range(2)]
    zero = jnp.zeros((16, LANES), bf16)

    def spread_row(ref, r, count=16):
        return jnp.broadcast_to(ref[pl.ds(r, 1), :], (count, LANES))

    def build(r, left_ref):
        base = spread_row(base_s, r).astype(bf16)
        group = spread_row(group_s, r).astype(bf16)
        weights = [spread_row(weight_s.at[place], r).astype(bf16) for place in range(4)]
        ahead = row16b - base
        wraps = ahead < 0
        place = jnp.where(wraps, ahead + 16, ahead)
        pattern = zero
        for k in range(4):
            pattern = jnp.where(place == k, weights[k], pattern)
        owner = jnp.where(wraps, group + 1, group)
        code = spread_row(code_s, r).astype(bf16)
        masks = [code == c for c in codes]
        for cell in range(WIN):
            expo = spread_row(term_s.at[cell], r, 8)
            claim = spread_row(term_s.at[WIN + cell], r, 8)
            both = jnp.concatenate([expo, claim], axis=0).astype(bf16)
            for half in range(2):
                left_ref[half * WIN + cell] = jnp.where(masks[half], both, zero)
        return jnp.concatenate(
            [jnp.where(owner == a, pattern, zero) for a in range(AGE // 16)], axis=0
        )

    def all_tiles(left_a, left_b, *accs):
        def fill(first, left, stage):
            for unit in range(2):
                ages = [
                    build(order_s[first + 4 * unit + j], left.at[4 * unit + j]) for j in range(4)
                ]
                pairs = [jnp.concatenate(ages[j : j + 2], axis=1) for j in (0, 2)]
                pltpu.matmul_push_rhs(
                    jnp.concatenate(pairs, axis=0), stage, unit, transpose=True
                )

        def multiply(left, stage):
            for pair in range(2):
                for unit in range(2):
                    j = 4 * unit + 2 * pair
                    rows = [left[j + k].reshape(ROWS, LANES) for k in range(2)]
                    pltpu.matmul_acc_lhs(
                        accs[2 * unit + pair],
                        jnp.concatenate(rows, axis=1),
                        load_staged_rhs=stage if pair == 0 else None,
                    )

        def take():
            totals = [pltpu.matmul_pop(acc) for acc in accs]
            return (totals[0][:, :AGE] + totals[1][:, AGE:]) + (
                totals[2][:, :AGE] + totals[3][:, AGE:]
            )

        fill(0, left_a, 0)

        def one_tile(t, done):
            steps = steps_s[t]
            odd = steps & 1

            @pl.when(steps > 0)
            def _():
                @pl.when(odd == 1)
                def _():
                    multiply(left_a, 0)
                    fill((done + 1) * STEP, left_a, 0)

                def two_steps(s, _):
                    first = (done + odd + 2 * s) * STEP
                    multiply(left_a, 0)
                    fill(first + STEP, left_b, 1)
                    multiply(left_b, 1)
                    fill(first + 2 * STEP, left_a, 0)
                    return 0

                lax.fori_loop(0, steps >> 1, two_steps, 0)
                total = take().reshape(2, WIN, 2, 8, LANES)
                for half in range(2):
                    for cell in range(WIN):
                        for channel in range(2):
                            acc_s[half * 2 + channel, t * DT + cell] += total[half, cell, channel]

            return done + steps

        lax.fori_loop(0, tiles, one_tile, jnp.int32(0))
        multiply(left_a, 0)
        acc_s[0, 0] = take()[:8]

    pl.run_scoped(
        all_tiles,
        *[pltpu.VMEM((STEP, ROWS // 16, 16, LANES), bf16)] * 2,
        *[pltpu.ACC(unit)((ROWS, MXU), f32) for unit in (0, 0, 1, 1)],
    )

    for copy in passed:
        copy.wait()
    low = lax.broadcasted_iota(jnp.int32, (8, LANES), 0) < 4
    mine = lax.axis_index("tile") & 1
    for whose, half in enumerate((mine, 1 - mine)):
        expo = acc_s[half * 2, 1 : dur + 1]
        claim = acc_s[half * 2 + 1, 1 : dur + 1]
        quarters = (
            jnp.where(low, expo, pltpu.roll(claim, 4, 1)),
            jnp.where(low, pltpu.roll(expo, 4, 1), claim),
        )
        for q in range(2):
            if whose == 0:
                keep_ref[q] = quarters[q]
            else:
                send_ref[pl.ds(q * dur, dur)] = quarters[q]
    for channel in range(2):
        pooled = jnp.sum(
            acc_s[channel, 1 : dur + 1] + acc_s[2 + channel, 1 : dur + 1], axis=1
        )
        base = 2 * dur + channel * (dur // 8)
        send_ref[pl.ds(base, dur // 8)] = pooled.reshape(dur // 8, 8, LANES)


def spread(tile_ids, fields, weights, tiles):
    blocks = tile_ids.shape[0]
    assert blocks % (SLAB * CHUNKS) == 0 and blocks % (LISTS * TALLY) == 0
    dur = tiles * DT
    rows = blocks + 8
    vmem = pl.BlockSpec(memory_space=pltpu.VMEM)
    smem = pl.BlockSpec(memory_space=pltpu.SMEM)
    hbm = pl.BlockSpec(memory_space=pltpu.HBM)
    return pl.pallas_call(
        functools.partial(spread_body, blocks, tiles),
        out_shape=(
            jax.ShapeDtypeStruct((2, dur, 8, LANES), f32),
            jax.ShapeDtypeStruct((2 * dur + 2 * (dur // 8), 8, LANES), f32),
            jax.ShapeDtypeStruct((3,) + weights[0].shape, f32),
        ),
        in_specs=[smem] + [hbm] * 10,
        out_specs=(vmem, vmem, vmem),
        scratch_shapes=[
            *[pltpu.VMEM((blocks, LANES), jnp.int32)] * 3,
            *[pltpu.VMEM((blocks, LANES), f32)] * 4,
            pltpu.VMEM((rows, LANES), f32),
            pltpu.VMEM((rows, LANES), f32),
            pltpu.VMEM((rows, LANES), f32),
            pltpu.VMEM((4, rows, LANES), f32),
            pltpu.VMEM((2 * WIN, rows, LANES), f32),
            pltpu.VMEM((4, dur + 3, 8, LANES), f32),
            pltpu.SMEM((blocks + STEP * tiles + 2 * STEP,), jnp.int32),
            *[pltpu.SMEM((tiles,), jnp.int32)] * (LISTS + 1),
            pltpu.SemaphoreType.DMA((CHUNKS + 1, 7)),
        ],
        compiler_params=pltpu.CompilerParams(vmem_limit_bytes=VMEM_SPREAD),
        name="spread",
    )(tile_ids, *fields, *weights)


def smooth_body(
    dur,
    weights_ref,
    grid_a_ref,
    grid_b_ref,
    pool_a_ref,
    pool_b_ref,
    out_ref,
    prior_s,
    x_s,
    r_s,
):
    half = dur // 2
    here = lax.axis_index("tile")
    slot, high = (here & 1) * 8 + (here & 2) * 2, here >> 2
    sub = lax.broadcasted_iota(jnp.int32, (8, LANES), 0)
    lane = lax.broadcasted_iota(jnp.int32, (1, 8, LANES), 2)
    low = sub < 4

    def swap(v):
        return pltpu.roll(v, 4, v.ndim - 2)

    def per_transition(which):
        every = jnp.broadcast_to(weights_ref[which], (8, weights_ref.shape[2]))
        at = lax.broadcasted_iota(jnp.int32, every.shape, 1)
        of = lax.broadcasted_iota(jnp.int32, every.shape, 0) & 3
        return jnp.sum(jnp.where(at == slot + of, every, 0.0), axis=1, keepdims=True)

    weight_a, weight_d, cred = map(per_transition, range(3))
    pool = pool_a_ref[...] + pool_b_ref[...]
    eighth = dur // 8
    prior_s[...] = (pool[eighth:] / (1.0 + pool[:eighth])).reshape(dur, LANES)
    grid = grid_a_ref[...] + grid_b_ref[...]
    top, bottom = grid[:half], grid[half:]
    diagonal = jnp.where(low, top, swap(bottom)) + cred
    claims = jnp.where(low, swap(top), bottom)
    prior = jnp.stack(
        [
            jnp.where(
                low,
                jnp.broadcast_to(prior_s[pl.ds(d, 1), :], (8, LANES)),
                jnp.broadcast_to(prior_s[pl.ds(half + d, 1), :], (8, LANES)),
            )
            for d in range(half)
        ]
    )
    rhs = claims + cred * prior

    def operate(v):
        y = v - 2.0 * pltpu.roll(v, LANES - 1, 2) + pltpu.roll(v, LANES - 2, 2)
        y = jnp.where(lane < AGE - 2, y, 0.0)
        along_age = y - 2.0 * pltpu.roll(y, 1, 2) + pltpu.roll(y, 2, 2)
        longer = jnp.concatenate([v, swap(v[:2])], axis=0)
        y = longer[:half] - 2.0 * longer[1 : half + 1] + longer[2 : half + 2]
        y = jnp.concatenate([y[: half - 2], jnp.where(low, y[half - 2 :], 0.0)], axis=0)
        longer = jnp.concatenate([jnp.where(low, 0.0, swap(y[half - 2 :])), y], axis=0)
        along_dur = longer[2:] - 2.0 * longer[1 : half + 1] + longer[:half]
        return diagonal * v + weight_a * along_age + weight_d * along_dur

    def inner(a, b):
        part = jnp.sum(a * b, axis=0)
        part = part + swap(part)
        return jnp.sum(part, axis=1, keepdims=True)

    x = jnp.zeros_like(rhs)
    r = rhs
    p = rhs
    norm = inner(r, r)
    for turn in range(ITERS):
        image = operate(p)
        alpha = norm / inner(p, image)
        x = x + alpha * p
        r = r - alpha * image
        if turn < ITERS - 1:
            after = inner(r, r)
            p = r + (after / norm) * p
            norm = after
    x_s[...] = x
    r_s[...] = r
    span = SHARE * DT
    in_low = high * span < half
    start = jnp.where(in_low, high * span, high * span - half)
    for dest in range(SHARE):
        for d in range(DT):
            xv = x_s[start + dest * DT + d]
            rv = r_s[start + dest * DT + d]
            row = jnp.where(
                in_low, jnp.where(low, xv, swap(rv)), jnp.where(low, swap(xv), rv)
            )
            out_ref[dest, pl.ds(d, 8, stride=DT), :] = row


def smooth(weights, grid_a, grid_b, pool_a, pool_b):
    dur = grid_a.shape[0]
    vmem = pl.BlockSpec(memory_space=pltpu.VMEM)
    return pl.pallas_call(
        functools.partial(smooth_body, dur),
        out_shape=jax.ShapeDtypeStruct((SHARE, 8 * DT, LANES), f32),
        in_specs=[vmem] * 5,
        out_specs=vmem,
        scratch_shapes=[
            pltpu.VMEM((dur, LANES), f32),
            pltpu.VMEM((dur // 2, 8, LANES), f32),
            pltpu.VMEM((dur // 2, 8, LANES), f32),
        ],
        compiler_params=pltpu.CompilerParams(vmem_limit_bytes=32 * 1024 * 1024),
        name="smooth",
    )(weights, grid_a, grid_b, pool_a, pool_b)


def gather_body(own_ref, one_ref, two_ref, three_ref, x_ref, r_ref):
    me = lax.axis_index("tile") & (SHARE - 1)
    for k, ref in enumerate((own_ref, one_ref, two_ref, three_ref)):
        other = me ^ k
        slot = (other & 1) * 2 + (other >> 1)
        got = ref[me] if k == 0 else ref[...]
        x_ref[slot] = got[: 4 * DT]
        r_ref[slot] = got[4 * DT :]


def gather(own, others):
    vmem = pl.BlockSpec(memory_space=pltpu.VMEM)
    shape = jax.ShapeDtypeStruct((SHARE, 4 * DT, LANES), f32)
    return pl.pallas_call(
        gather_body,
        out_shape=(shape, shape),
        in_specs=[vmem] * 4,
        out_specs=(vmem, vmem),
        compiler_params=pltpu.CompilerParams(vmem_limit_bytes=4 * 1024 * 1024),
        name="gather",
    )(own, *others)


def swap_with(value, axis, bit):
    size = lax.axis_size(axis)
    return lax.ppermute(value, axis, [(i, i ^ bit) for i in range(size)])


def bits_of(size):
    bits = [1 << k for k in range(size.bit_length() - 1)]
    assert 1 << len(bits) == size, size
    return bits


def per_device(
    age_cell,
    dur_cell,
    trans_code,
    age_frac,
    dur_frac,
    exposure,
    claims,
    block_tile,
    smooth_age,
    smooth_dur,
    credibility,
):
    trans_dev = smooth_age.shape[0]
    tiles = lax.axis_size("tile")
    groups = lax.axis_size("tg")
    dur = tiles * DT
    assert trans_dev == 4 * SHARE and tiles % 8 == 0
    here = lax.axis_index("tile")
    near = (here >> 1) & 1
    tile_ids = pltpu.with_memory_space_constraint(block_tile.reshape(-1), pltpu.HBM)
    blocks = tile_ids.shape[0]
    fields = [
        pltpu.with_memory_space_constraint(field.reshape(blocks, LANES), pltpu.HBM)
        for field in (age_cell, dur_cell, trans_code, age_frac, dur_frac, exposure, claims)
    ]
    weights = [
        pltpu.with_memory_space_constraint(weight.reshape(1, -1), pltpu.HBM)
        for weight in (smooth_age, smooth_dur, credibility)
    ]
    keep, send, weights = spread(tile_ids, fields, weights, tiles)
    got = swap_with(send, "tile", 1)
    pool = send[2 * dur :] + got[2 * dur :]
    got = got[: 2 * dur].reshape(keep.shape)

    def quarter(at):
        return lax.dynamic_index_in_dim(keep, at, 0, False) + lax.dynamic_index_in_dim(
            got, at, 0, False
        )

    tile_bits = bits_of(tiles)
    pool_bits = [("tile", bit) for bit in tile_bits[1:]] + [("tg", bit) for bit in bits_of(groups)]

    def pool_step(k, value):
        return swap_with(value, *pool_bits[k])

    def grid_step(k, value):
        return swap_with(value, "tile", tile_bits[k])

    grid = quarter(near) + grid_step(1, quarter(1 - near))
    last = len(pool_bits) - 1
    for k in range(last):
        pool = pool + pool_step(k, pool)
    pool_other = pool_step(last, pool)
    for k in range(2, len(tile_bits) - 1):
        grid = grid + grid_step(k, grid)
    grid_other = grid_step(len(tile_bits) - 1, grid)
    own = smooth(
        weights,
        grid,
        grid_other,
        pool,
        pool_other,
    )
    me = here & (SHARE - 1)
    others = [
        swap_with(lax.dynamic_index_in_dim(own, me ^ k, 0, False), "tile", k) for k in (1, 2, 3)
    ]
    smoothed, residual = gather(own, others)
    shape = (trans_dev, DT, AGE)
    return smoothed.reshape(shape), residual.reshape(shape)


def solution(mesh):
    records = P("tg", "tile")
    in_specs = (records,) * 7 + (P("tg", "tile", None),) + (P("tg"),) * 3
    out_specs = (P("tg", "tile", None), P("tg", "tile", None))
    mapped = jax.shard_map(
        per_device, mesh=mesh, in_specs=in_specs, out_specs=out_specs, check_vma=False
    )

    def run(*args):
        with jax.sharding.use_abstract_mesh(mesh.abstract_mesh):
            return mapped(*args)

    return run
```

```python
import functools

import jax
import jax.numpy as jnp
from jax import lax
from jax.experimental import pallas as pl
from jax.experimental.pallas import tpu as pltpu
from jax.sharding import PartitionSpec as P


AGE = 128
DT = 4
ITERS = 4
LANES = 128
WIN = DT + 3
MXU = 256
STEP = 8
SHARE = 4
ROWS = 2 * WIN * 16
CHUNKS = 2
LISTS = 4
SLAB = 32
TALLY = 8
VMEM_SPREAD = 40 * 1024 * 1024


f32 = jnp.float32
bf16 = jnp.bfloat16


def spline(frac):
    rest = 1.0 - frac
    cube = frac * frac * frac
    return (
        rest * rest * rest / 6.0,
        (3.0 * cube - 6.0 * frac * frac + 4.0) / 6.0,
        (-3.0 * cube + 3.0 * frac * frac + 3.0 * frac + 1.0) / 6.0,
        cube / 6.0,
    )


def spread_body(
    blocks,
    tiles,
    tile_ref,
    age_hbm,
    off_hbm,
    code_hbm,
    age_frac_hbm,
    dur_frac_hbm,
    expo_hbm,
    claim_hbm,
    age_w_hbm,
    dur_w_hbm,
    cred_hbm,
    keep_ref,
    send_ref,
    weights_ref,
    cells_s,
    values_s,
    table_s,
    acc_s,
    order_s,
    steps_s,
    *places_and_sems,
):
    at, sems = places_and_sems[:LISTS], places_and_sems[LISTS]
    base_s, group_s, code_s = (table_s.at[k] for k in range(3))
    weight_s, term_s = table_s.at[pl.ds(3, 4)], table_s.at[pl.ds(7, 2 * WIN)]
    dur = tiles * DT
    part = blocks // CHUNKS
    quarter = blocks // LISTS
    sources = (age_hbm, off_hbm, code_hbm, age_frac_hbm, dur_frac_hbm, expo_hbm, claim_hbm)
    age_ref, off_ref, code_ref = (cells_s.at[k] for k in range(3))
    age_frac_ref, dur_frac_ref, expo_ref, claim_ref = (values_s.at[k] for k in range(4))
    targets = (age_ref, off_ref, code_ref, age_frac_ref, dur_frac_ref, expo_ref, claim_ref)
    copies = []
    for c in range(CHUNKS):
        rows = pl.ds(c * part, part)
        copies.append(
            [
                pltpu.make_async_copy(source.at[rows], target.at[rows], sems.at[c, k])
                for k, (source, target) in enumerate(zip(sources, targets))
            ]
        )
        for copy in copies[-1]:
            copy.start()

    passed = [
        pltpu.make_async_copy(source, weights_ref.at[k], sems.at[CHUNKS, k])
        for k, source in enumerate((age_w_hbm, dur_w_hbm, cred_hbm))
    ]
    for copy in passed:
        copy.start()

    def clear(t, _):
        for place in at:
            place[t] = 0
        return 0

    lax.fori_loop(0, tiles, clear, 0)

    def tally(i, _):
        for j in range(TALLY):
            for k, place in enumerate(at):
                t = tile_ref[k * quarter + i * TALLY + j]
                place[t] = place[t] + 1
        return 0

    lax.fori_loop(0, quarter // TALLY, tally, 0)

    def starts(t, start):
        end = start
        for place in at:
            count = place[t]
            place[t] = end
            end = end + count
        for j in range(STEP - 1):
            order_s[end + j] = blocks
        steps = lax.div(end - start + (STEP - 1), STEP)
        steps_s[t] = steps
        return start + steps * STEP

    padded = lax.fori_loop(0, tiles, starts, jnp.int32(0))
    for j in range(STEP):
        order_s[padded + j] = blocks

    acc_s[...] = jnp.zeros_like(acc_s)
    blank = jnp.zeros((8, LANES), f32)
    pad = pl.ds(blocks, 8)
    base_s[pad] = blank
    group_s[pad] = blank
    code_s[pad] = blank - 1.0
    for place in range(4):
        weight_s[place, pad] = blank
    for row in range(2 * WIN):
        term_s[row, pad] = blank

    def prepare(i, _):
        rows = pl.ds(pl.multiple_of(i * SLAB, SLAB), SLAB)
        first = age_ref[rows] - 1
        base_s[rows] = (first & 15).astype(f32)
        group_s[rows] = (first >> 4).astype(f32)
        code_s[rows] = code_ref[rows].astype(f32)
        for place, weight in enumerate(spline(age_frac_ref[rows])):
            weight_s[place, rows] = weight.astype(bf16).astype(f32)
        dur_w = spline(dur_frac_ref[rows])
        offset = off_ref[rows]
        is_offset = [offset == o for o in range(DT)]
        for channel, value in enumerate((expo_ref[rows], claim_ref[rows])):
            terms = [(w * value).astype(bf16).astype(f32) for w in dur_w]
            for cell in range(WIN):
                term = jnp.zeros((SLAB, LANES), f32)
                for o in range(DT):
                    if 0 <= cell - o < 4:
                        term = jnp.where(is_offset[o], terms[cell - o], term)
                term_s[channel * WIN + cell, rows] = term
        for j in range(SLAB // LISTS):
            for k, place in enumerate(at):
                block = k * quarter + i * (SLAB // LISTS) + j
                t = tile_ref[block]
                spot = place[t]
                order_s[spot] = block
                place[t] = spot + 1
        return 0

    for c in range(CHUNKS):
        for copy in copies[c]:
            copy.wait()
        lax.fori_loop(c * (part // SLAB), (c + 1) * (part // SLAB), prepare, 0)

    row16 = lax.broadcasted_iota(jnp.int32, (16, LANES), 0)
    row16b = row16.astype(f32).astype(bf16)
    codes = [(half * 8 + (row16 & 7)).astype(f32).astype(bf16) for half in range(2)]
    zero = jnp.zeros((16, LANES), bf16)

    def spread_row(ref, r, count=16):
        return jnp.broadcast_to(ref[pl.ds(r, 1), :], (count, LANES))

    def build(r, left_ref):
        base = spread_row(base_s, r).astype(bf16)
        group = spread_row(group_s, r).astype(bf16)
        weights = [spread_row(weight_s.at[place], r).astype(bf16) for place in range(4)]
        ahead = row16b - base
        wraps = ahead < 0
        place = jnp.where(wraps, ahead + 16, ahead)
        pattern = zero
        for k in range(4):
            pattern = jnp.where(place == k, weights[k], pattern)
        owner = jnp.where(wraps, group + 1, group)
        code = spread_row(code_s, r).astype(bf16)
        masks = [code == c for c in codes]
        for cell in range(WIN):
            expo = spread_row(term_s.at[cell], r, 8)
            claim = spread_row(term_s.at[WIN + cell], r, 8)
            both = jnp.concatenate([expo, claim], axis=0).astype(bf16)
            for half in range(2):
                left_ref[half * WIN + cell] = jnp.where(masks[half], both, zero)
        return jnp.concatenate(
            [jnp.where(owner == a, pattern, zero) for a in range(AGE // 16)], axis=0
        )

    def all_tiles(left_a, left_b, *accs):
        def fill(first, left, stage):
            for unit in range(2):
                ages = [
                    build(order_s[first + 4 * unit + j], left.at[4 * unit + j]) for j in range(4)
                ]
                pairs = [jnp.concatenate(ages[j : j + 2], axis=1) for j in (0, 2)]
                pltpu.matmul_push_rhs(
                    jnp.concatenate(pairs, axis=0), stage, unit, transpose=True
                )

        def multiply(left, stage):
            for pair in range(2):
                for unit in range(2):
                    j = 4 * unit + 2 * pair
                    rows = [left[j + k].reshape(ROWS, LANES) for k in range(2)]
                    pltpu.matmul_acc_lhs(
                        accs[2 * unit + pair],
                        jnp.concatenate(rows, axis=1),
                        load_staged_rhs=stage if pair == 0 else None,
                    )

        def take():
            totals = [pltpu.matmul_pop(acc) for acc in accs]
            return (totals[0][:, :AGE] + totals[1][:, AGE:]) + (
                totals[2][:, :AGE] + totals[3][:, AGE:]
            )

        fill(0, left_a, 0)

        def one_tile(t, done):
            steps = steps_s[t]
            odd = steps & 1

            @pl.when(steps > 0)
            def _():
                @pl.when(odd == 1)
                def _():
                    multiply(left_a, 0)
                    fill((done + 1) * STEP, left_a, 0)

                def two_steps(s, _):
                    first = (done + odd + 2 * s) * STEP
                    multiply(left_a, 0)
                    fill(first + STEP, left_b, 1)
                    multiply(left_b, 1)
                    fill(first + 2 * STEP, left_a, 0)
                    return 0

                lax.fori_loop(0, steps >> 1, two_steps, 0)
                total = take().reshape(2, WIN, 2, 8, LANES)
                for half in range(2):
                    for cell in range(WIN):
                        for channel in range(2):
                            acc_s[half * 2 + channel, t * DT + cell] += total[half, cell, channel]

            return done + steps

        lax.fori_loop(0, tiles, one_tile, jnp.int32(0))
        multiply(left_a, 0)
        acc_s[0, 0] = take()[:8]

    pl.run_scoped(
        all_tiles,
        *[pltpu.VMEM((STEP, ROWS // 16, 16, LANES), bf16)] * 2,
        *[pltpu.ACC(unit)((ROWS, MXU), f32) for unit in (0, 0, 1, 1)],
    )

    for copy in passed:
        copy.wait()
    low = lax.broadcasted_iota(jnp.int32, (8, LANES), 0) < 4
    mine = lax.axis_index("tile") & 1
    for whose, half in enumerate((mine, 1 - mine)):
        expo = acc_s[half * 2, 1 : dur + 1]
        claim = acc_s[half * 2 + 1, 1 : dur + 1]
        quarters = (
            jnp.where(low, expo, pltpu.roll(claim, 4, 1)),
            jnp.where(low, pltpu.roll(expo, 4, 1), claim),
        )
        for q in range(2):
            if whose == 0:
                keep_ref[q] = quarters[q]
            else:
                send_ref[pl.ds(q * dur, dur)] = quarters[q]
    for channel in range(2):
        pooled = jnp.sum(
            acc_s[channel, 1 : dur + 1] + acc_s[2 + channel, 1 : dur + 1], axis=1
        )
        base = 2 * dur + channel * (dur // 8)
        send_ref[pl.ds(base, dur // 8)] = pooled.reshape(dur // 8, 8, LANES)


def spread(tile_ids, fields, weights, tiles):
    blocks = tile_ids.shape[0]
    assert blocks % (SLAB * CHUNKS) == 0 and blocks % (LISTS * TALLY) == 0
    dur = tiles * DT
    rows = blocks + 8
    vmem = pl.BlockSpec(memory_space=pltpu.VMEM)
    smem = pl.BlockSpec(memory_space=pltpu.SMEM)
    hbm = pl.BlockSpec(memory_space=pltpu.HBM)
    return pl.pallas_call(
        functools.partial(spread_body, blocks, tiles),
        out_shape=(
            jax.ShapeDtypeStruct((2, dur, 8, LANES), f32),
            jax.ShapeDtypeStruct((2 * dur + 2 * (dur // 8), 8, LANES), f32),
            jax.ShapeDtypeStruct((3,) + weights[0].shape, f32),
        ),
        in_specs=[smem] + [hbm] * 10,
        out_specs=(vmem, vmem, vmem),
        scratch_shapes=[
            pltpu.VMEM((3, blocks, LANES), jnp.int32),
            pltpu.VMEM((4, blocks, LANES), f32),
            pltpu.VMEM((7 + 2 * WIN, rows, LANES), f32),
            pltpu.VMEM((4, dur + 3, 8, LANES), f32),
            pltpu.SMEM((blocks + STEP * tiles + 2 * STEP,), jnp.int32),
            *[pltpu.SMEM((tiles,), jnp.int32)] * (LISTS + 1),
            pltpu.SemaphoreType.DMA((CHUNKS + 1, 7)),
        ],
        compiler_params=pltpu.CompilerParams(vmem_limit_bytes=VMEM_SPREAD),
        name="spread",
    )(tile_ids, *fields, *weights)


def smooth_body(
    dur,
    weights_ref,
    grid_a_ref,
    grid_b_ref,
    pool_a_ref,
    pool_b_ref,
    out_ref,
    prior_s,
    x_s,
    r_s,
):
    half = dur // 2
    here = lax.axis_index("tile")
    slot, high = (here & 1) * 8 + (here & 2) * 2, here >> 2
    sub = lax.broadcasted_iota(jnp.int32, (8, LANES), 0)
    lane = lax.broadcasted_iota(jnp.int32, (1, 8, LANES), 2)
    low = sub < 4

    def swap(v):
        return pltpu.roll(v, 4, v.ndim - 2)

    def per_transition(which):
        every = jnp.broadcast_to(weights_ref[which], (8, weights_ref.shape[2]))
        at = lax.broadcasted_iota(jnp.int32, every.shape, 1)
        of = lax.broadcasted_iota(jnp.int32, every.shape, 0) & 3
        return jnp.sum(jnp.where(at == slot + of, every, 0.0), axis=1, keepdims=True)

    weight_a, weight_d, cred = map(per_transition, range(3))
    pool = pool_a_ref[...] + pool_b_ref[...]
    eighth = dur // 8
    prior_s[...] = (pool[eighth:] / (1.0 + pool[:eighth])).reshape(dur, LANES)
    grid = grid_a_ref[...] + grid_b_ref[...]
    top, bottom = grid[:half], grid[half:]
    diagonal = jnp.where(low, top, swap(bottom)) + cred
    claims = jnp.where(low, swap(top), bottom)
    prior = jnp.stack(
        [
            jnp.where(
                low,
                jnp.broadcast_to(prior_s[pl.ds(d, 1), :], (8, LANES)),
                jnp.broadcast_to(prior_s[pl.ds(half + d, 1), :], (8, LANES)),
            )
            for d in range(half)
        ]
    )
    rhs = claims + cred * prior

    def operate(v):
        y = v - 2.0 * pltpu.roll(v, LANES - 1, 2) + pltpu.roll(v, LANES - 2, 2)
        y = jnp.where(lane < AGE - 2, y, 0.0)
        along_age = y - 2.0 * pltpu.roll(y, 1, 2) + pltpu.roll(y, 2, 2)
        longer = jnp.concatenate([v, swap(v[:2])], axis=0)
        y = longer[:half] - 2.0 * longer[1 : half + 1] + longer[2 : half + 2]
        y = jnp.concatenate([y[: half - 2], jnp.where(low, y[half - 2 :], 0.0)], axis=0)
        longer = jnp.concatenate([jnp.where(low, 0.0, swap(y[half - 2 :])), y], axis=0)
        along_dur = longer[2:] - 2.0 * longer[1 : half + 1] + longer[:half]
        return diagonal * v + weight_a * along_age + weight_d * along_dur

    def inner(a, b):
        part = jnp.sum(a * b, axis=0)
        part = part + swap(part)
        return jnp.sum(part, axis=1, keepdims=True)

    x = jnp.zeros_like(rhs)
    r = rhs
    p = rhs
    norm = inner(r, r)
    for turn in range(ITERS):
        image = operate(p)
        alpha = norm / inner(p, image)
        x = x + alpha * p
        r = r - alpha * image
        if turn < ITERS - 1:
            after = inner(r, r)
            p = r + (after / norm) * p
            norm = after
    x_s[...] = x
    r_s[...] = r
    span = SHARE * DT
    in_low = high * span < half
    start = jnp.where(in_low, high * span, high * span - half)
    for dest in range(SHARE):
        for d in range(DT):
            xv = x_s[start + dest * DT + d]
            rv = r_s[start + dest * DT + d]
            row = jnp.where(
                in_low, jnp.where(low, xv, swap(rv)), jnp.where(low, swap(xv), rv)
            )
            out_ref[dest, pl.ds(d, 8, stride=DT), :] = row


def smooth(weights, grid_a, grid_b, pool_a, pool_b):
    dur = grid_a.shape[0]
    vmem = pl.BlockSpec(memory_space=pltpu.VMEM)
    return pl.pallas_call(
        functools.partial(smooth_body, dur),
        out_shape=jax.ShapeDtypeStruct((SHARE, 8 * DT, LANES), f32),
        in_specs=[vmem] * 5,
        out_specs=vmem,
        scratch_shapes=[
            pltpu.VMEM((dur, LANES), f32),
            pltpu.VMEM((dur // 2, 8, LANES), f32),
            pltpu.VMEM((dur // 2, 8, LANES), f32),
        ],
        compiler_params=pltpu.CompilerParams(vmem_limit_bytes=32 * 1024 * 1024),
        name="smooth",
    )(weights, grid_a, grid_b, pool_a, pool_b)


def gather_body(own_ref, one_ref, two_ref, three_ref, x_ref, r_ref):
    me = lax.axis_index("tile") & (SHARE - 1)
    for k, ref in enumerate((own_ref, one_ref, two_ref, three_ref)):
        other = me ^ k
        slot = (other & 1) * 2 + (other >> 1)
        got = ref[me] if k == 0 else ref[...]
        x_ref[slot] = got[: 4 * DT]
        r_ref[slot] = got[4 * DT :]


def gather(own, others):
    vmem = pl.BlockSpec(memory_space=pltpu.VMEM)
    shape = jax.ShapeDtypeStruct((SHARE, 4 * DT, LANES), f32)
    return pl.pallas_call(
        gather_body,
        out_shape=(shape, shape),
        in_specs=[vmem] * 4,
        out_specs=(vmem, vmem),
        compiler_params=pltpu.CompilerParams(vmem_limit_bytes=4 * 1024 * 1024),
        name="gather",
    )(own, *others)


def swap_with(value, axis, bit):
    size = lax.axis_size(axis)
    return lax.ppermute(value, axis, [(i, i ^ bit) for i in range(size)])


def bits_of(size):
    bits = [1 << k for k in range(size.bit_length() - 1)]
    assert 1 << len(bits) == size, size
    return bits


def per_device(
    age_cell,
    dur_cell,
    trans_code,
    age_frac,
    dur_frac,
    exposure,
    claims,
    block_tile,
    smooth_age,
    smooth_dur,
    credibility,
):
    trans_dev = smooth_age.shape[0]
    tiles = lax.axis_size("tile")
    groups = lax.axis_size("tg")
    dur = tiles * DT
    assert trans_dev == 4 * SHARE and tiles % 8 == 0
    here = lax.axis_index("tile")
    near = (here >> 1) & 1
    tile_ids = pltpu.with_memory_space_constraint(block_tile.reshape(-1), pltpu.HBM)
    blocks = tile_ids.shape[0]
    fields = [
        pltpu.with_memory_space_constraint(field.reshape(blocks, LANES), pltpu.HBM)
        for field in (age_cell, dur_cell, trans_code, age_frac, dur_frac, exposure, claims)
    ]
    weights = [
        pltpu.with_memory_space_constraint(weight.reshape(1, -1), pltpu.HBM)
        for weight in (smooth_age, smooth_dur, credibility)
    ]
    keep, send, weights = spread(tile_ids, fields, weights, tiles)
    got = swap_with(send, "tile", 1)
    pool = send[2 * dur :] + got[2 * dur :]
    got = got[: 2 * dur].reshape(keep.shape)

    def quarter(at):
        return lax.dynamic_index_in_dim(keep, at, 0, False) + lax.dynamic_index_in_dim(
            got, at, 0, False
        )

    tile_bits = bits_of(tiles)
    pool_bits = [("tile", bit) for bit in tile_bits[1:]] + [("tg", bit) for bit in bits_of(groups)]

    def pool_step(k, value):
        return swap_with(value, *pool_bits[k])

    def grid_step(k, value):
        return swap_with(value, "tile", tile_bits[k])

    grid = quarter(near) + grid_step(1, quarter(1 - near))
    last = len(pool_bits) - 1
    for k in range(last):
        pool = pool + pool_step(k, pool)
    pool_other = pool_step(last, pool)
    for k in range(2, len(tile_bits) - 1):
        grid = grid + grid_step(k, grid)
    grid_other = grid_step(len(tile_bits) - 1, grid)
    own = smooth(
        weights,
        grid,
        grid_other,
        pool,
        pool_other,
    )
    me = here & (SHARE - 1)
    others = [
        swap_with(lax.dynamic_index_in_dim(own, me ^ k, 0, False), "tile", k) for k in (1, 2, 3)
    ]
    smoothed, residual = gather(own, others)
    shape = (trans_dev, DT, AGE)
    return smoothed.reshape(shape), residual.reshape(shape)


def solution(mesh):
    records = P("tg", "tile")
    in_specs = (records,) * 7 + (P("tg", "tile", None),) + (P("tg"),) * 3
    out_specs = (P("tg", "tile", None), P("tg", "tile", None))
    mapped = jax.shard_map(
        per_device, mesh=mesh, in_specs=in_specs, out_specs=out_specs, check_vma=False
    )

    def run(*args):
        with jax.sharding.use_abstract_mesh(mesh.abstract_mesh):
            return mapped(*args)

    return run
```
